32 devices in a mesh: groups: 2 (over y), seq: 4 (over z), head: 4 (over x, core).
Axes of the slice: x: 2, y: 2, z: 4, core: 2. Of those that a mesh axis runs over, the one named last changes fastest.
Arguments:
- tile_rows: bfloat16 [8192, 1536], P(('groups', 'seq', 'head')), parts along dimension 0, may hold values from -6 to 6
- tile_route: int32 [8192, 2], P(('groups', 'seq', 'head')), parts along dimension 0, may hold values from 0 to 255, as said below
- embed_weight: bfloat16 [1536, 768], replicated, may hold values from -0.15625 to 0.15625
- norm_gain: float32 [768], replicated, may hold values from 0.1 to 1.9
- qkv_weight: bfloat16 [768, 16, 3, 48], P(None, 'head'), may hold values from -1 to 1
- out_weight: bfloat16 [768, 768], P('head'), may hold values from -0.21875 to 0.21875
Outputs:
- mixed: bfloat16 [8192, 768], P(('groups', 'seq', 'head')), parts along dimension 0
The draws below stay inside these ranges and needn't reach their ends.
There are 2 independent parts, one for each index of `groups`. The reference program is written for one: setup_inputs(seed, part) draws one part's arguments, and reference() takes and returns one part's arrays. A program takes and returns all parts, laid end to end along the dimension named above; an argument that names none is the same for every part. Nothing has to cross between parts.
Inputs may be any that keep to these rules, and one draw needn't show every extreme that they name: `tile_route`: A tile's owner holds the same head class as the tile's own device. From one device at most 128 tiles go to one index of seq, and some device sends exactly 128 to one index in every draw; every slot of every owner receives exactly one tile.
All inputs are finite; a program needn't handle non-finite values.
Results may differ from the reference program's by a relative error of at most 0.0075.
Values may be sent and summed in bfloat16 or wider, within the bound.
A program may use at most 64 MiB of HBM per device.

```python
import jax
import jax.numpy as jnp
from jax import lax

D_IN = 1536
D = 768
HEADS = 16
HEAD_DIM = 48
TILES_DEV = 1024
TILES = 4096
IN_DEV = 256
CAP = 128
N_SEQ = 4
N_HEAD = 4


def route_table(key):
    count_seq = N_SEQ
    per_device = IN_DEV
    capacity = CAP
    shift_count = count_seq // 2 + 1

    def one_class(class_key):
        key_shift, key_split, key_source, key_target = jax.random.split(class_key, 4)
        shifts = jax.random.permutation(key_shift, count_seq)[:shift_count].astype(jnp.int32)
        extra = jax.random.randint(key_split, (), 1, capacity).astype(jnp.int32)
        loads = jnp.concatenate([jnp.full((shift_count - 2,), capacity, jnp.int32), jnp.stack([extra, capacity - extra])])
        ends = jnp.cumsum(loads)
        places = jnp.arange(per_device, dtype=jnp.int32)
        block = jnp.sum((places[:, None] >= ends[None, :]).astype(jnp.int32), axis=1)
        source_keys = jax.random.split(key_source, count_seq)
        order = jax.vmap(lambda sub: jax.random.permutation(sub, per_device))(source_keys).astype(jnp.int32)
        target_keys = jax.random.split(key_target, count_seq)
        slot_perm = jax.vmap(lambda sub: jax.random.permutation(sub, per_device))(target_keys).astype(jnp.int32)
        sources = jnp.arange(count_seq, dtype=jnp.int32)[:, None]
        owner = (sources + shifts[block[order]]) % count_seq
        slot_index = slot_perm[owner, order]
        return (owner, slot_index)
    class_keys = jax.random.split(key, N_HEAD)
    owner, slot_index = jax.vmap(one_class)(class_keys)
    owner = jnp.transpose(owner, (1, 0, 2)).reshape(-1)
    slot_index = jnp.transpose(slot_index, (1, 0, 2)).reshape(-1)
    return jnp.stack([owner, slot_index], axis=1).astype(jnp.int32)


def draw_tile_route(key, part):
    return route_table(jax.random.fold_in(key, 11))


def draw_qkv_weight(key, part):
    key_base = jax.random.fold_in(jax.random.fold_in(key, 23), 0)
    base = jax.random.normal(key_base, (D, HEADS, 3, HEAD_DIM), jnp.float32)
    weight = base * (1.5 * D ** (-0.5))
    return jnp.clip(weight, -1.0, 1.0).astype(jnp.bfloat16)


def levels(own_key, shape, shards, low, high):
    level = 1.0
    for dim, shards_of in shards:
        steps = jax.random.uniform(jax.random.fold_in(jax.random.fold_in(own_key, 6), dim), (shards_of,), jnp.float32, low / len(shards), high / len(shards))
        level = level * jnp.repeat(jnp.exp(steps), shape[dim] // shards_of).reshape((-1,) + (1,) * (len(shape) - 1 - dim))
    return level


def normal_values(own_key, extent, deviation, limit, shards=(), kind=jnp.bfloat16):
    values = deviation * jax.random.normal(own_key, extent, jnp.float32)
    if shards:
        values = values * levels(own_key, extent, shards, -0.22, 0.18)
    return jnp.clip(values, -limit, limit).astype(kind)


def setup_inputs(seed: int = 0, part: int = 0) -> dict:
    key_of = jax.random.split(jax.random.key(seed), 7)
    part_keys = jax.random.split(jax.random.fold_in(key_of[6], part), 7)
    return {
        "tile_rows": normal_values(part_keys[0], (TILES, D_IN), 1.0, 6.0, ((0, 16),)),
        "tile_route": draw_tile_route(jax.random.fold_in(jax.random.fold_in(key_of[6], part), 71), part),
        "embed_weight": normal_values(key_of[2], (D_IN, D), D_IN ** -0.5, 0.15625),
        "norm_gain": jnp.clip(1.0 + 0.18 * jax.random.normal(key_of[3], (D,), jnp.float32), 0.1, 1.9),
        "qkv_weight": draw_qkv_weight(jax.random.fold_in(key_of[6], 71), part),
        "out_weight": normal_values(key_of[5], (D, D), D ** -0.5, 0.21875, ((0, 4),)),
    }


EPSILON = 1e-05
DILATIONS = (1, 4, 16)
FRACTIONS = (16, 4, 1)

def layer_norm(rows, gain):
    rows = rows.astype(jnp.float32)
    row_mean = lax.optimization_barrier(jnp.mean(rows, axis=-1, keepdims=True))
    centered = rows - row_mean
    row_var = lax.optimization_barrier(jnp.mean(centered * centered, axis=-1, keepdims=True))
    return (centered * lax.rsqrt(row_var + EPSILON) * gain.astype(jnp.float32)).astype(jnp.bfloat16)

def attend_block(queries, key_rows, values):
    score_scale = queries.shape[-1] ** (-0.5)
    scores = jnp.dot(queries, key_rows.T, preferred_element_type=jnp.float32) * score_scale
    row_max = lax.optimization_barrier(jnp.max(scores, axis=-1))
    expo = jnp.exp(scores - row_max[:, None])
    denominator = lax.optimization_barrier(jnp.sum(expo, axis=-1))
    weights = (expo / denominator[:, None]).astype(jnp.bfloat16)
    head_out = jnp.dot(weights, values, preferred_element_type=jnp.float32)
    return (head_out, row_max + jnp.log(denominator))

def expand_rows(head_out, log_total, offset, dilation):
    count = head_out.shape[0]
    pick_mask = jnp.arange(dilation, dtype=jnp.int32) == offset
    full_out = jnp.where(pick_mask[None, :, None], head_out[:, None, :], 0.0).reshape(count * dilation, -1)
    full_total = jnp.where(pick_mask[None, :], log_total[:, None], -1e+30).reshape(count * dilation)
    return (full_out, full_total)

def merge_scales(outputs, totals):
    row_max = jnp.maximum(jnp.maximum(totals[0], totals[1]), totals[2])
    numer = jnp.zeros_like(outputs[0])
    denom = jnp.zeros_like(totals[0])
    for full_out, full_total in zip(outputs, totals):
        factor = jnp.exp(full_total - row_max)
        numer = numer + factor[:, None] * full_out
        denom = denom + factor
    return numer / denom[:, None]

def one_head(head_index, qkv_head):
    outputs = []
    totals = []
    head_dim = qkv_head.shape[-1]
    for fraction, dilation in zip(FRACTIONS, DILATIONS):
        segment = TILES // fraction
        offset = (head_index % dilation).astype(jnp.int32)
        shaped = qkv_head.reshape(TILES // dilation, dilation, 3, head_dim)
        picked = lax.dynamic_index_in_dim(shaped, offset, axis=1, keepdims=False)
        grouped = picked.reshape(TILES // segment, segment // dilation, 3, head_dim)
        head_out, log_total = lax.map(lambda block_in: attend_block(block_in[:, 0], block_in[:, 1], block_in[:, 2]), grouped)
        full_out, full_total = expand_rows(head_out.reshape(TILES // dilation, head_dim), log_total.reshape(TILES // dilation), offset, dilation)
        outputs.append(full_out)
        totals.append(full_total)
    return merge_scales(outputs, totals).astype(jnp.bfloat16)

def reference(tile_rows, tile_route, embed_weight, norm_gain, qkv_weight, out_weight):
    projected = jnp.dot(tile_rows, embed_weight, preferred_element_type=jnp.float32).astype(jnp.bfloat16)
    position = jnp.arange(TILES, dtype=jnp.int32)
    head_class = position // IN_DEV % N_HEAD
    target = tile_route[:, 0] * TILES_DEV + head_class * IN_DEV + tile_route[:, 1]
    embedded = jnp.zeros((TILES, D), jnp.bfloat16).at[target].set(projected)
    normed = layer_norm(embedded, norm_gain)
    qkv = jnp.dot(normed, qkv_weight.reshape(D, -1), preferred_element_type=jnp.float32).astype(jnp.bfloat16)
    qkv = qkv.reshape(TILES, HEADS, 3, HEAD_DIM).transpose(1, 0, 2, 3)
    heads_out = lax.map(lambda pair: one_head(pair[0], pair[1]), (jnp.arange(HEADS, dtype=jnp.int32), qkv))
    attention = heads_out.transpose(1, 0, 2).reshape(TILES, D)
    mixed = embedded.astype(jnp.float32) + jnp.dot(attention, out_weight, preferred_element_type=jnp.float32)
    return mixed.astype(jnp.bfloat16)
```

```python
import functools

import jax
import jax.numpy as jnp
from jax import lax
from jax.experimental import pallas as pl
from jax.experimental.pallas import tpu as pltpu
from jax.sharding import PartitionSpec as P

EPSILON = 1e-05
DILATIONS = (1, 4, 16)
FRACTIONS = (16, 4, 1)


def from_partner(block, axis, apart):
    count = lax.axis_size(axis)
    route = []
    for low in range(count):
        high = low | 1 << apart
        if high != low and high < count:
            route += [(low, high), (high, low)]
    return lax.ppermute(block, axis, route)


def layer_norm(rows, gain):
    row_mean = jnp.mean(rows, axis=-1, keepdims=True)
    centered = rows - row_mean
    row_var = jnp.mean(centered * centered, axis=-1, keepdims=True)
    return (centered * lax.rsqrt(row_var + EPSILON) * gain).astype(jnp.bfloat16)


def attend_block(queries, key_rows, values):
    score_scale = queries.shape[-1] ** (-0.5)
    scores = jnp.dot(queries, key_rows.T, preferred_element_type=jnp.float32) * score_scale
    row_max = jnp.max(scores, axis=-1)
    expo = jnp.exp(scores - row_max[:, None])
    denominator = jnp.sum(expo, axis=-1)
    weights = (expo / denominator[:, None]).astype(jnp.bfloat16)
    head_out = jnp.dot(weights, values, preferred_element_type=jnp.float32)
    return (head_out, row_max + jnp.log(denominator))


def attend(queries, key_rows, values):
    count = queries.shape[0]
    if count > 512 and count % 512 == 0:
        blocks = queries.reshape(count // 512, 512, queries.shape[1])
        head_out, log_total = lax.map(
            lambda block_in: attend_block(block_in, key_rows, values), blocks
        )
        return (head_out.reshape(count, -1), log_total.reshape(count))
    return attend_block(queries, key_rows, values)


def expand_rows(head_out, log_total, offset, dilation):
    count = head_out.shape[0]
    pick_mask = jnp.arange(dilation, dtype=jnp.int32) == offset
    full_out = jnp.where(pick_mask[None, :, None], head_out[:, None, :], 0.0).reshape(
        count * dilation, -1
    )
    full_total = jnp.where(pick_mask[None, :], log_total[:, None], -1e30).reshape(count * dilation)
    return (full_out, full_total)


def merge_scales(outputs, totals):
    row_max = jnp.maximum(jnp.maximum(totals[0], totals[1]), totals[2])
    numer = jnp.zeros_like(outputs[0])
    denom = jnp.zeros_like(totals[0])
    for full_out, full_total in zip(outputs, totals):
        factor = jnp.exp(full_total - row_max)
        numer = numer + factor[:, None] * full_out
        denom = denom + factor
    return numer / denom[:, None]


def collect_segment(flat_rows, levels, seq_index):
    for level in range(levels):
        partner = from_partner(flat_rows, "seq", level)
        upper_half = seq_index >> level & 1 == 1
        lower_rows = jnp.where(upper_half, partner, flat_rows)
        upper_rows = jnp.where(upper_half, flat_rows, partner)
        flat_rows = jnp.concatenate([lower_rows, upper_rows], axis=0)
    return flat_rows


def local(tile_rows, tile_route, embed_weight, norm_gain, qkv_weight, out_weight):
    seq_count = lax.axis_size("seq")
    seq_index = lax.axis_index("seq")
    in_rows = tile_rows.shape[0]
    width = embed_weight.shape[1]
    capacity = 2 * in_rows // seq_count
    projected = jnp.dot(tile_rows, embed_weight, preferred_element_type=jnp.float32).astype(
        jnp.bfloat16
    )
    dest_seq = tile_route[:, 0]
    slot_index = tile_route[:, 1]
    owner_hits = (dest_seq[:, None] == jnp.arange(seq_count, dtype=jnp.int32)[None, :]).astype(
        jnp.int32
    )
    earlier = jnp.cumsum(owner_hits, axis=0) - owner_hits
    owner_rank = jnp.sum(earlier * owner_hits, axis=1)
    buffer_place = dest_seq * capacity + owner_rank
    send_pick = jnp.arange(seq_count * capacity, dtype=jnp.int32)[:, None] == buffer_place[None, :]
    outgoing = jnp.dot(
        send_pick.astype(jnp.bfloat16), projected, preferred_element_type=jnp.float32
    ).astype(jnp.bfloat16)
    outgoing_slot = jnp.sum(jnp.where(send_pick, slot_index[None, :] + 1, 0), axis=1)
    arrived, arrived_slot = (
        lax.all_to_all(
            outgoing.reshape(seq_count, capacity, width),
            "seq",
            split_axis=0,
            concat_axis=0,
            tiled=True,
        ),
        lax.all_to_all(
            outgoing_slot.reshape(seq_count, capacity),
            "seq",
            split_axis=0,
            concat_axis=0,
            tiled=True,
        ),
    )
    landing = jnp.arange(in_rows, dtype=jnp.int32)[:, None] + 1 == arrived_slot.reshape(-1)[None, :]
    embedded = jnp.dot(
        landing.astype(jnp.bfloat16), arrived.reshape(-1, width), preferred_element_type=jnp.float32
    )
    normed = layer_norm(embedded, norm_gain)
    heads_here = qkv_weight.shape[1]
    head_dim = qkv_weight.shape[3]
    weight_flat = qkv_weight.reshape(width, -1)
    qkv = jnp.dot(
        lax.all_gather(normed, "head", axis=0, tiled=True),
        weight_flat,
        preferred_element_type=jnp.float32,
    ).astype(jnp.bfloat16)
    rows_here = qkv.shape[0]
    qkv = qkv.reshape(rows_here, heads_here, 3, head_dim)
    first_head = lax.axis_index("head") * heads_here
    total_rows = rows_here * seq_count
    outputs = [[] for member in range(heads_here)]
    totals = [[] for member in range(heads_here)]
    for fraction, dilation in zip(FRACTIONS, DILATIONS):
        segment = total_rows // fraction
        per_segment = segment // dilation
        count = rows_here // dilation
        shaped = qkv.reshape(count, dilation, heads_here, 3, head_dim)
        offsets = []
        chosen = []
        for member in range(heads_here):
            offset = (first_head + member) % dilation
            offsets.append(offset)
            chosen.append(
                lax.dynamic_index_in_dim(shaped[:, :, member], offset, axis=1, keepdims=False)
            )
        chosen = jnp.stack(chosen, axis=1)
        queries = chosen[:, :, 0]
        pairs = chosen[:, :, 1:]
        if segment > rows_here:
            levels = (segment // rows_here).bit_length() - 1
            flat_rows = collect_segment(pairs.reshape(count, -1), levels, seq_index)
            pairs = flat_rows.reshape(per_segment, heads_here, 2, head_dim)
            groups = 1
        else:
            groups = rows_here // segment
        grouped_queries = queries.reshape(groups, count // groups, heads_here, head_dim)
        grouped_pairs = pairs.reshape(groups, per_segment, heads_here, 2, head_dim)
        for member in range(heads_here):
            head_out, log_total = lax.map(
                lambda block_in: attend(block_in[0], block_in[1][:, 0], block_in[1][:, 1]),
                (grouped_queries[:, :, member], grouped_pairs[:, :, member]),
            )
            full_out, full_total = expand_rows(
                head_out.reshape(count, head_dim),
                log_total.reshape(count),
                offsets[member],
                dilation,
            )
            outputs[member].append(full_out)
            totals[member].append(full_total)
    merged = [
        merge_scales(outputs[member], totals[member]).astype(jnp.bfloat16)
        for member in range(heads_here)
    ]
    attention = jnp.stack(merged, axis=1).reshape(rows_here, heads_here * head_dim)
    regrouped = lax.all_to_all(attention, "head", split_axis=0, concat_axis=1, tiled=True)
    branch = jnp.dot(
        regrouped,
        lax.all_gather(out_weight, "head", axis=0, tiled=True),
        preferred_element_type=jnp.float32,
    )
    return (embedded + branch).astype(jnp.bfloat16)


MESH = pl.DeviceIdType.MESH
LOWEST = -1e30


def dot_nt(a, b):
    return lax.dot_general(a, b, (((1,), (1,)), ((), ())), preferred_element_type=jnp.float32)


def dot(a, b):
    return jnp.dot(a, b, preferred_element_type=jnp.float32)


def iota(shape, dim):
    return lax.broadcasted_iota(jnp.int32, shape, dim)


def layer_kernel(
    dims,
    tile_any,
    route_ref,
    embed_any,
    gain_ref,
    w_any,
    wo_any,
    out_ref,
    tile_v,
    embed_v,
    wt,
    wo_v,
    outgoing,
    arrived,
    slot_out,
    slot_in,
    emb,
    qs,
    kvs,
    kv2,
    kx3,
    kv3,
    num,
    top,
    den,
    load_sem,
    local_sem,
    w_send,
    w_recv,
    route_send,
    route_recv,
    slot_send,
    slot_recv,
    kv2_send,
    kv2_recv,
    kx3_send,
    kx3_recv,
    kv3_send,
    kv3_recv,
):
    S, H, R, D, NC, M, E, SH, d2, d3 = dims
    cap = arrived.shape[2]
    cols = arrived.shape[3]
    G = M * E
    p2 = R // d2
    p3 = R // d3
    v_low = G // 128 * 128
    VW = 2 * G - v_low
    lead = G - v_low
    scale = E ** (-0.5)
    s = lax.axis_index("seq")
    c = lax.axis_index("head")
    near = c + 1 - 2 * (c % 2)
    far = (c + 2) % H
    near_far = (near + 2) % H
    seq_to = [(s + k) % S for k in range(S)]
    seq_from = [(s + S - k) % S for k in range(S)]

    loads = [pltpu.make_async_copy(tile_any, tile_v, load_sem.at[0])]
    for n in range(NC):
        loads.append(
            pltpu.make_async_copy(
                embed_any.at[:, pl.ds(n * cols, cols)], embed_v.at[n], load_sem.at[1 + n]
            )
        )
    for copy in loads:
        copy.start()

    barrier = pltpu.get_barrier_semaphore()
    for k in range(1, S):
        pl.semaphore_signal(barrier, inc=1, device_id={"seq": seq_to[k]}, device_id_type=MESH)
    for peer in (near, far):
        pl.semaphore_signal(barrier, inc=1, device_id={"head": peer}, device_id_type=MESH)

    dest = route_ref[0:1, :]
    slot = route_ref[1:2, :]
    sub = max(8, S)
    hits = iota((sub, R), 0) == dest
    hits_f = jnp.where(hits, 1.0, 0.0)
    below = jnp.where(iota((R, R), 0) < iota((R, R), 1), 1.0, 0.0).astype(jnp.bfloat16)
    earlier = dot(hits_f.astype(jnp.bfloat16), below)
    rank = jnp.sum(earlier * hits_f, axis=0, keepdims=True).astype(jnp.int32)
    place = dest * cap + rank
    pick = jnp.where(iota((S * cap, R), 0) == place, 1.0, 0.0).astype(jnp.bfloat16)
    slot_f = jnp.broadcast_to((slot + 1).astype(jnp.float32), (8, R)).astype(jnp.bfloat16)
    slot_rows = dot_nt(slot_f, pick).astype(jnp.int32)
    for t in range(S):
        slot_out[t] = slot_rows[:, t * cap : (t + 1) * cap]

    pl.semaphore_wait(barrier, S - 1 + 2)

    def remote(src, dst, send, recv, **device):
        copy = pltpu.make_async_remote_copy(
            src_ref=src,
            dst_ref=dst,
            send_sem=send,
            recv_sem=recv,
            device_id=device,
            device_id_type=MESH,
        )
        return copy

    slot_copies = []
    for k in range(1, S):
        copy = remote(
            slot_out.at[seq_to[k]], slot_in.at[s], slot_send.at[k], slot_recv.at[k], seq=seq_to[k]
        )
        copy.start()
        slot_copies.append(copy)
    slot_in[s] = slot_out[s]

    w_far, w_near, w_local = [], [], []
    for x in range(4):
        source = w_any.at[:, x] if x < 3 else wo_any
        target = wt.at[c, x] if x < 3 else wo_v.at[c]
        w_far.append(remote(source, target, w_send.at[0, x], w_recv.at[0, x], head=far))
        w_near.append(remote(source, target, w_send.at[1, x], w_recv.at[1, x], head=near))
        w_local.append(pltpu.make_async_copy(source, target, local_sem.at[x]))

    def w_relay(x):
        ref = wt.at[far, x] if x < 3 else wo_v.at[far]
        return remote(ref, ref, w_send.at[2, x], w_recv.at[2, x], head=near)

    for x in range(4):
        w_far[x].start()
    loads[0].wait()
    route_copies = []
    for n in range(NC):
        loads[1 + n].wait()
        projected = dot(tile_v[...], embed_v[n]).astype(jnp.bfloat16)
        outgoing[n] = dot(pick, projected).astype(jnp.bfloat16).reshape(S, cap, cols)
        row = []
        for k in range(1, S):
            copy = remote(
                outgoing.at[n, seq_to[k]],
                arrived.at[n, s],
                route_send.at[n, k],
                route_recv.at[n, k],
                seq=seq_to[k],
            )
            copy.start()
            row.append(copy)
        route_copies.append(row)
        arrived[n, s] = outgoing[n, s]
    for x in range(4):
        w_local[x].start()
        w_near[x].start()

    def original(position):
        return (position % p3) * d3 + ((position // p3) % (d3 // d2)) * d2 + position // p2

    for copy in slot_copies:
        copy.wait_recv()
    slots = jnp.concatenate([slot_in[t][0:1, :] for t in range(S)], axis=1)
    landing = jnp.where(original(iota((R, S * cap), 0)) + 1 == slots, 1.0, 0.0).astype(jnp.bfloat16)
    back = jnp.where(original(iota((R, R), 1)) == iota((R, R), 0), 1.0, 0.0).astype(jnp.bfloat16)

    relays = [w_relay(x) for x in range(4)]
    parts = []
    for n in range(NC):
        if n < 3:
            w_far[n].wait_recv()
            relays[n].start()
        for copy in route_copies[n]:
            copy.wait_recv()
        parts.append(dot(landing, arrived[n].reshape(S * cap, cols)))
    embedded = jnp.concatenate(parts, axis=1)
    emb[...] = embedded.astype(jnp.bfloat16)
    normed = layer_norm(embedded, gain_ref[...])

    w_relay_in = [
        remote(ref, ref, w_send.at[2, x], w_recv.at[2, x], head=near)
        for x, ref in enumerate([wt.at[near_far, y] for y in range(3)] + [wo_v.at[near_far]])
    ]
    for x in (1, 2, 0):
        w_local[x].wait()
        w_near[x].wait_recv()
        w_relay_in[x].wait_recv()
    lane_head = (iota((p2, 2 * G), 1) % G) // E
    for g in range(SH):
        kv = dot_nt(normed, wt[g, 1:3].reshape(2 * G, D))
        kvs[g] = kv.astype(jnp.bfloat16)
        chosen = kv[0:p2]
        for m in range(1, M):
            chosen = jnp.where(lane_head == m, kv[m * p2 : (m + 1) * p2], chosen)
        chosen = chosen.astype(jnp.bfloat16)
        kv2[c, g] = chosen
        kx3[g] = chosen[g * p3 : (g + 1) * p3]
    kv2_far = remote(kv2.at[c], kv2.at[c], kv2_send.at[0], kv2_recv.at[0], head=far)
    kv2_near = remote(kv2.at[c], kv2.at[c], kv2_send.at[1], kv2_recv.at[1], head=near)
    kv2_relay = remote(kv2.at[far], kv2.at[far], kv2_send.at[2], kv2_recv.at[2], head=near)
    kv2_relay_in = remote(
        kv2.at[near_far], kv2.at[near_far], kv2_send.at[2], kv2_recv.at[2], head=near
    )
    kx3_copies = []
    for k in range(1, S):
        copy = remote(kx3, kv3.at[s, c], kx3_send.at[k], kx3_recv.at[k], seq=seq_to[k])
        copy.start()
        kx3_copies.append(copy)
    kv2_far.start()
    kv2_near.start()
    for g in range(SH):
        qs[g] = dot_nt(normed, wt[g, 0].reshape(G, D)).astype(jnp.bfloat16)

    q_head = iota((R, G), 1) // E
    v_head = (iota((R, VW), 1) - lead + 2 * E) // E - 2

    def scale_one(g, carry):
        queries = qs[g]
        keys = kvs[g, :, 0:G]
        values = kvs[g, :, v_low : 2 * G]
        numer = jnp.zeros((R, VW), jnp.float32)
        peak = jnp.zeros((R, VW), jnp.float32)
        denom = jnp.ones((R, VW), jnp.float32)
        for m in range(M):
            mask = jnp.where(q_head == m, 1.0, 0.0).astype(jnp.bfloat16)
            scores = dot_nt(queries * mask, keys)
            row_max = jnp.max(scores, axis=-1, keepdims=True)
            expo = jnp.exp((scores - row_max) * scale)
            total = jnp.sum(expo, axis=-1, keepdims=True)
            head_out = dot(expo.astype(jnp.bfloat16), values)
            mine = v_head == m
            numer = jnp.where(mine, head_out, numer)
            peak = jnp.where(mine, row_max, peak)
            denom = jnp.where(mine, total, denom)
        num[g] = numer
        top[g] = peak
        den[g] = denom
        return carry

    lax.fori_loop(0, SH - 1, scale_one, 0)
    w_far[3].wait_recv()
    relays[3].start()
    kv2_far.wait_recv()
    kv2_relay.start()
    kv3_far, kv3_near, kv3_relay, kv3_relay_in = [], [], [], []
    for k in range(1, S):
        kx3_copies[k - 1].wait_recv()
        block = kv3.at[seq_from[k], c]
        kv3_far.append(remote(block, block, kv3_send.at[0, k], kv3_recv.at[0, k], head=far))
        kv3_near.append(remote(block, block, kv3_send.at[1, k], kv3_recv.at[1, k], head=near))
        kv3_far[-1].start()
        kv3_near[-1].start()
        block = kv3.at[seq_from[k], far]
        kv3_relay.append(remote(block, block, kv3_send.at[2, k], kv3_recv.at[2, k], head=near))
        block = kv3.at[seq_from[k], near_far]
        kv3_relay_in.append(remote(block, block, kv3_send.at[2, k], kv3_recv.at[2, k], head=near))
    lax.fori_loop(SH - 1, SH, scale_one, 0)

    kv2_near.wait_recv()
    kv2_relay_in.wait_recv()

    def merge(g, rows, mine, row_max, total, head_out):
        old = top[g, rows, :]
        this = jnp.where(mine, row_max, LOWEST)
        peak = jnp.maximum(old, this)
        keep = jnp.exp((old - peak) * scale)
        add = jnp.where(mine, jnp.exp((this - peak) * scale), 0.0)
        top[g, rows, :] = peak
        num[g, rows, :] = num[g, rows, :] * keep + head_out * add
        den[g, rows, :] = den[g, rows, :] * keep + total * add

    q_diag = jnp.where(q_head == iota((R, G), 0) // p2, 1.0, 0.0).astype(jnp.bfloat16)
    v_diag = v_head == iota((R, VW), 0) // p2

    def scale_two(g, carry):
        keys = kv2[:, g, :, 0:G].reshape(H * p2, G)
        values = kv2[:, g, :, v_low : 2 * G].reshape(H * p2, VW)
        scores = dot_nt(qs[g] * q_diag, keys)
        row_max = jnp.max(scores, axis=-1, keepdims=True)
        expo = jnp.exp((scores - row_max) * scale)
        total = jnp.sum(expo, axis=-1, keepdims=True)
        head_out = dot(expo.astype(jnp.bfloat16), values)
        merge(g, pl.ds(0, R), v_diag, row_max, total, head_out)
        return carry

    lax.fori_loop(0, SH, scale_two, 0)
    for k in range(1, S):
        kv3_far[k - 1].wait_recv()
        kv3_relay[k - 1].start()
    for g in range(SH):
        for other in range(H):
            kv3[s, other, g] = kv2[other, g, g * p3 : (g + 1) * p3, :]
    residual = dot(back, emb[...])
    for k in range(1, S):
        kv3_near[k - 1].wait_recv()
        kv3_relay_in[k - 1].wait_recv()

    q_small = jnp.where(
        iota((M * p3, G), 1) // E == iota((M * p3, G), 0) // p3, 1.0, 0.0
    ).astype(jnp.bfloat16)

    def scale_three(g, carry):
        starts = [pl.multiple_of(m * p2 + g * p3, p3) for m in range(M)]
        queries = jnp.concatenate([qs[g, pl.ds(start, p3), :] for start in starts], axis=0)
        keys = kv3[:, :, g, :, 0:G].reshape(S * H * p3, G)
        values = kv3[:, :, g, :, v_low : 2 * G].reshape(S * H * p3, VW)
        scores = dot_nt(queries * q_small, keys)
        row_max = jnp.max(scores, axis=-1, keepdims=True)
        expo = jnp.exp((scores - row_max) * scale)
        total = jnp.sum(expo, axis=-1, keepdims=True)
        head_out = dot(expo.astype(jnp.bfloat16), values)
        for m in range(M):
            part = slice(m * p3, (m + 1) * p3)
            merge(
                g,
                pl.ds(starts[m], p3),
                (iota((p3, VW), 1) >= lead + m * E) & (iota((p3, VW), 1) < lead + (m + 1) * E),
                row_max[part],
                total[part],
                head_out[part],
            )
        return carry

    lax.fori_loop(0, SH, scale_three, 0)

    w_local[3].wait()
    w_near[3].wait_recv()
    w_relay_in[3].wait_recv()
    mixed = residual
    for g in range(SH):
        attention = (num[g] / den[g]).astype(jnp.bfloat16)
        ordered = dot(back, attention)[:, lead:VW].astype(jnp.bfloat16)
        mixed = mixed + dot(ordered, wo_v[g])
    out_ref[...] = mixed.astype(jnp.bfloat16)

    sent = slot_copies + w_far + w_near + relays + [kv2_far, kv2_near, kv2_relay] + kx3_copies
    sent += kv3_far + kv3_near + kv3_relay
    for row in route_copies:
        sent += row
    for copy in sent:
        copy.wait_send()


def fused(tile_rows, tile_route, embed_weight, norm_gain, qkv_weight, out_weight):
    S = lax.axis_size("seq")
    H = lax.axis_size("head")
    R, d_in = tile_rows.shape
    D = embed_weight.shape[1]
    M, E = qkv_weight.shape[1], qkv_weight.shape[3]
    G = M * E
    cap = 2 * R // S
    NC = D // 256
    SH = H
    d2, d3 = DILATIONS[1:]
    p2, p3 = R // d2, R // d3
    VW = 2 * G - G // 128 * 128
    bf, f32 = jnp.bfloat16, jnp.float32
    any_spec = pl.BlockSpec(memory_space=pl.ANY)
    vmem = pl.BlockSpec(memory_space=pltpu.VMEM)
    dma = pltpu.SemaphoreType.DMA
    return pl.pallas_call(
        functools.partial(layer_kernel, (S, H, R, D, NC, M, E, SH, d2, d3)),
        out_shape=jax.ShapeDtypeStruct((R, D), bf),
        in_specs=[any_spec, vmem, any_spec, vmem, any_spec, any_spec],
        out_specs=vmem,
        scratch_shapes=[
            pltpu.VMEM((R, d_in), bf),
            pltpu.VMEM((NC, d_in, 256), bf),
            pltpu.VMEM((H, 3, M, E, D), bf),
            pltpu.VMEM((H, G, D), bf),
            pltpu.VMEM((NC, S, cap, 256), bf),
            pltpu.VMEM((NC, S, cap, 256), bf),
            pltpu.VMEM((S, 8, cap), jnp.int32),
            pltpu.VMEM((S, 8, cap), jnp.int32),
            pltpu.VMEM((R, D), bf),
            pltpu.VMEM((SH, R, G), bf),
            pltpu.VMEM((SH, R, 2 * G), bf),
            pltpu.VMEM((H, SH, p2, 2 * G), bf),
            pltpu.VMEM((SH, p3, 2 * G), bf),
            pltpu.VMEM((S, H, SH, p3, 2 * G), bf),
            pltpu.VMEM((SH, R, VW), f32),
            pltpu.VMEM((SH, R, VW), f32),
            pltpu.VMEM((SH, R, VW), f32),
            dma((1 + NC,)),
            dma((4,)),
            dma((3, 4)),
            dma((3, 4)),
            dma((NC, S)),
            dma((NC, S)),
            dma((S,)),
            dma((S,)),
            dma((3,)),
            dma((3,)),
            dma((S,)),
            dma((S,)),
            dma((3, S)),
            dma((3, S)),
        ],
        compiler_params=pltpu.CompilerParams(
            collective_id=0, has_side_effects=True, vmem_limit_bytes=56 * 1024 * 1024
        ),
    )(
        tile_rows,
        tile_route.T,
        embed_weight,
        norm_gain.reshape(1, D),
        qkv_weight.transpose(1, 2, 3, 0),
        out_weight,
    )


def fits(mesh):
    def check(tile_rows, embed_weight, qkv_weight):
        S, H = mesh.shape["seq"], mesh.shape["head"]
        rows = tile_rows.shape[0] // mesh.size
        heads = qkv_weight.shape[1] // H
        d2, d3 = DILATIONS[1:]
        return (
            H == 4
            and heads == d2
            and heads * H == d3
            and FRACTIONS[0] == S * H
            and FRACTIONS[1] == S
            and FRACTIONS[2] == 1
            and rows % (16 * d3) == 0
            and rows <= 256
            and embed_weight.shape[1] % 256 == 0
            and embed_weight.shape[1] // 256 >= 3
        )

    return check


def solution(mesh):
    check = fits(mesh)

    def program(tile_rows, tile_route, embed_weight, norm_gain, qkv_weight, out_weight):
        body = fused if check(tile_rows, embed_weight, qkv_weight) else local
        return jax.shard_map(
            body,
            mesh=mesh,
            in_specs=(
                P(("groups", "seq", "head"), None),
                P(("groups", "seq", "head"), None),
                P(),
                P(),
                P(None, "head", None, None),
                P("head", None),
            ),
            out_specs=P(("groups", "seq", "head"), None),
            check_vma=False,
        )(tile_rows, tile_route, embed_weight, norm_gain, qkv_weight, out_weight)

    return program
```

```python
import functools

import jax
import jax.numpy as jnp
from jax import lax
from jax.experimental import pallas as pl
from jax.experimental.pallas import tpu as pltpu
from jax.sharding import PartitionSpec as P

EPSILON = 1e-05
DILATIONS = (1, 4, 16)
FRACTIONS = (16, 4, 1)


def from_partner(block, axis, apart):
    count = lax.axis_size(axis)
    route = []
    for low in range(count):
        high = low | 1 << apart
        if high != low and high < count:
            route += [(low, high), (high, low)]
    return lax.ppermute(block, axis, route)


def layer_norm(rows, gain):
    row_mean = jnp.mean(rows, axis=-1, keepdims=True)
    centered = rows - row_mean
    row_var = jnp.mean(centered * centered, axis=-1, keepdims=True)
    return (centered * lax.rsqrt(row_var + EPSILON) * gain).astype(jnp.bfloat16)


def attend_block(queries, key_rows, values):
    score_scale = queries.shape[-1] ** (-0.5)
    scores = jnp.dot(queries, key_rows.T, preferred_element_type=jnp.float32) * score_scale
    row_max = jnp.max(scores, axis=-1)
    expo = jnp.exp(scores - row_max[:, None])
    denominator = jnp.sum(expo, axis=-1)
    weights = (expo / denominator[:, None]).astype(jnp.bfloat16)
    head_out = jnp.dot(weights, values, preferred_element_type=jnp.float32)
    return (head_out, row_max + jnp.log(denominator))


def attend(queries, key_rows, values):
    count = queries.shape[0]
    if count > 512 and count % 512 == 0:
        blocks = queries.reshape(count // 512, 512, queries.shape[1])
        head_out, log_total = lax.map(
            lambda block_in: attend_block(block_in, key_rows, values), blocks
        )
        return (head_out.reshape(count, -1), log_total.reshape(count))
    return attend_block(queries, key_rows, values)


def expand_rows(head_out, log_total, offset, dilation):
    count = head_out.shape[0]
    pick_mask = jnp.arange(dilation, dtype=jnp.int32) == offset
    full_out = jnp.where(pick_mask[None, :, None], head_out[:, None, :], 0.0).reshape(
        count * dilation, -1
    )
    full_total = jnp.where(pick_mask[None, :], log_total[:, None], -1e30).reshape(count * dilation)
    return (full_out, full_total)


def merge_scales(outputs, totals):
    row_max = jnp.maximum(jnp.maximum(totals[0], totals[1]), totals[2])
    numer = jnp.zeros_like(outputs[0])
    denom = jnp.zeros_like(totals[0])
    for full_out, full_total in zip(outputs, totals):
        factor = jnp.exp(full_total - row_max)
        numer = numer + factor[:, None] * full_out
        denom = denom + factor
    return numer / denom[:, None]


def collect_segment(flat_rows, levels, seq_index):
    for level in range(levels):
        partner = from_partner(flat_rows, "seq", level)
        upper_half = seq_index >> level & 1 == 1
        lower_rows = jnp.where(upper_half, partner, flat_rows)
        upper_rows = jnp.where(upper_half, flat_rows, partner)
        flat_rows = jnp.concatenate([lower_rows, upper_rows], axis=0)
    return flat_rows


def local(tile_rows, tile_route, embed_weight, norm_gain, qkv_weight, out_weight):
    seq_count = lax.axis_size("seq")
    seq_index = lax.axis_index("seq")
    in_rows = tile_rows.shape[0]
    width = embed_weight.shape[1]
    capacity = 2 * in_rows // seq_count
    projected = jnp.dot(tile_rows, embed_weight, preferred_element_type=jnp.float32).astype(
        jnp.bfloat16
    )
    dest_seq = tile_route[:, 0]
    slot_index = tile_route[:, 1]
    owner_hits = (dest_seq[:, None] == jnp.arange(seq_count, dtype=jnp.int32)[None, :]).astype(
        jnp.int32
    )
    earlier = jnp.cumsum(owner_hits, axis=0) - owner_hits
    owner_rank = jnp.sum(earlier * owner_hits, axis=1)
    buffer_place = dest_seq * capacity + owner_rank
    send_pick = jnp.arange(seq_count * capacity, dtype=jnp.int32)[:, None] == buffer_place[None, :]
    outgoing = jnp.dot(
        send_pick.astype(jnp.bfloat16), projected, preferred_element_type=jnp.float32
    ).astype(jnp.bfloat16)
    outgoing_slot = jnp.sum(jnp.where(send_pick, slot_index[None, :] + 1, 0), axis=1)
    arrived, arrived_slot = (
        lax.all_to_all(
            outgoing.reshape(seq_count, capacity, width),
            "seq",
            split_axis=0,
            concat_axis=0,
            tiled=True,
        ),
        lax.all_to_all(
            outgoing_slot.reshape(seq_count, capacity),
            "seq",
            split_axis=0,
            concat_axis=0,
            tiled=True,
        ),
    )
    landing = jnp.arange(in_rows, dtype=jnp.int32)[:, None] + 1 == arrived_slot.reshape(-1)[None, :]
    embedded = jnp.dot(
        landing.astype(jnp.bfloat16), arrived.reshape(-1, width), preferred_element_type=jnp.float32
    )
    normed = layer_norm(embedded, norm_gain)
    heads_here = qkv_weight.shape[1]
    head_dim = qkv_weight.shape[3]
    weight_flat = qkv_weight.reshape(width, -1)
    qkv = jnp.dot(
        lax.all_gather(normed, "head", axis=0, tiled=True),
        weight_flat,
        preferred_element_type=jnp.float32,
    ).astype(jnp.bfloat16)
    rows_here = qkv.shape[0]
    qkv = qkv.reshape(rows_here, heads_here, 3, head_dim)
    first_head = lax.axis_index("head") * heads_here
    total_rows = rows_here * seq_count
    outputs = [[] for member in range(heads_here)]
    totals = [[] for member in range(heads_here)]
    for fraction, dilation in zip(FRACTIONS, DILATIONS):
        segment = total_rows // fraction
        per_segment = segment // dilation
        count = rows_here // dilation
        shaped = qkv.reshape(count, dilation, heads_here, 3, head_dim)
        offsets = []
        chosen = []
        for member in range(heads_here):
            offset = (first_head + member) % dilation
            offsets.append(offset)
            chosen.append(
                lax.dynamic_index_in_dim(shaped[:, :, member], offset, axis=1, keepdims=False)
            )
        chosen = jnp.stack(chosen, axis=1)
        queries = chosen[:, :, 0]
        pairs = chosen[:, :, 1:]
        if segment > rows_here:
            levels = (segment // rows_here).bit_length() - 1
            flat_rows = collect_segment(pairs.reshape(count, -1), levels, seq_index)
            pairs = flat_rows.reshape(per_segment, heads_here, 2, head_dim)
            groups = 1
        else:
            groups = rows_here // segment
        grouped_queries = queries.reshape(groups, count // groups, heads_here, head_dim)
        grouped_pairs = pairs.reshape(groups, per_segment, heads_here, 2, head_dim)
        for member in range(heads_here):
            head_out, log_total = lax.map(
                lambda block_in: attend(block_in[0], block_in[1][:, 0], block_in[1][:, 1]),
                (grouped_queries[:, :, member], grouped_pairs[:, :, member]),
            )
            full_out, full_total = expand_rows(
                head_out.reshape(count, head_dim),
                log_total.reshape(count),
                offsets[member],
                dilation,
            )
            outputs[member].append(full_out)
            totals[member].append(full_total)
    merged = [
        merge_scales(outputs[member], totals[member]).astype(jnp.bfloat16)
        for member in range(heads_here)
    ]
    attention = jnp.stack(merged, axis=1).reshape(rows_here, heads_here * head_dim)
    regrouped = lax.all_to_all(attention, "head", split_axis=0, concat_axis=1, tiled=True)
    branch = jnp.dot(
        regrouped,
        lax.all_gather(out_weight, "head", axis=0, tiled=True),
        preferred_element_type=jnp.float32,
    )
    return (embedded + branch).astype(jnp.bfloat16)


MESH = pl.DeviceIdType.MESH
LOWEST = -1e30


def dot_nt(a, b):
    return lax.dot_general(a, b, (((1,), (1,)), ((), ())), preferred_element_type=jnp.float32)


def dot(a, b):
    return jnp.dot(a, b, preferred_element_type=jnp.float32)


def iota(shape, dim):
    return lax.broadcasted_iota(jnp.int32, shape, dim)


def layer_kernel(
    dims,
    tile_any,
    route_ref,
    embed_any,
    gain_ref,
    w_any,
    wo_any,
    out_ref,
    tile_v,
    embed_v,
    wt,
    wo_v,
    outgoing,
    arrived,
    slot_out,
    slot_in,
    emb,
    qs,
    kvs,
    kv2,
    kx3,
    kv3,
    num,
    top,
    den,
    load_sem,
    local_sem,
    w_send,
    w_recv,
    route_send,
    route_recv,
    slot_send,
    slot_recv,
    kv2_send,
    kv2_recv,
    kx3_send,
    kx3_recv,
    kv3_send,
    kv3_recv,
):
    S, H, R, D, NC, M, E, SH, d2, d3 = dims
    cap = arrived.shape[2]
    cols = arrived.shape[3]
    G = M * E
    p2 = R // d2
    p3 = R // d3
    v_low = G // 128 * 128
    VW = 2 * G - v_low
    lead = G - v_low
    scale = E ** (-0.5)
    s = lax.axis_index("seq")
    c = lax.axis_index("head")
    side = lax.axis_index("groups")
    across = 1 - side
    near = c + 1 - 2 * (c % 2)
    far = (c + 2) % H
    near_far = (near + 2) % H
    seq_to = [(s + k) % S for k in range(S)]
    seq_from = [(s + S - k) % S for k in range(S)]

    loads = [pltpu.make_async_copy(tile_any, tile_v, load_sem.at[0])]
    for n in range(NC):
        loads.append(
            pltpu.make_async_copy(
                embed_any.at[:, pl.ds(n * cols, cols)], embed_v.at[n], load_sem.at[1 + n]
            )
        )
    for copy in loads:
        copy.start()

    barrier = pltpu.get_barrier_semaphore()
    for k in range(1, S):
        pl.semaphore_signal(barrier, inc=1, device_id={"seq": seq_to[k]}, device_id_type=MESH)
    for peer in (near, far):
        pl.semaphore_signal(barrier, inc=1, device_id={"head": peer}, device_id_type=MESH)
    pl.semaphore_signal(barrier, inc=1, device_id={"groups": across}, device_id_type=MESH)

    dest = route_ref[0:1, :]
    slot = route_ref[1:2, :]
    sub = max(8, S)
    hits = iota((sub, R), 0) == dest
    hits_f = jnp.where(hits, 1.0, 0.0)
    below = jnp.where(iota((R, R), 0) < iota((R, R), 1), 1.0, 0.0).astype(jnp.bfloat16)
    earlier = dot(hits_f.astype(jnp.bfloat16), below)
    rank = jnp.sum(earlier * hits_f, axis=0, keepdims=True).astype(jnp.int32)
    place = dest * cap + rank
    pick = jnp.where(iota((S * cap, R), 0) == place, 1.0, 0.0).astype(jnp.bfloat16)
    slot_f = jnp.broadcast_to((slot + 1).astype(jnp.float32), (8, R)).astype(jnp.bfloat16)
    slot_rows = dot_nt(slot_f, pick).astype(jnp.int32)
    for t in range(S):
        slot_out[t] = slot_rows[:, t * cap : (t + 1) * cap]

    pl.semaphore_wait(barrier, S - 1 + 3)

    def remote(src, dst, send, recv, **device):
        copy = pltpu.make_async_remote_copy(
            src_ref=src,
            dst_ref=dst,
            send_sem=send,
            recv_sem=recv,
            device_id=device,
            device_id_type=MESH,
        )
        return copy

    slot_copies = []
    for k in range(1, S):
        copy = remote(
            slot_out.at[seq_to[k]], slot_in.at[s], slot_send.at[k], slot_recv.at[k], seq=seq_to[k]
        )
        copy.start()
        slot_copies.append(copy)
    slot_in[s] = slot_out[s]

    half_m, half_g = M // 2, G // 2

    def w_block(owner, x):
        return wt.at[owner, x] if x < 3 else wo_v.at[owner]

    def w_half(owner, x, part):
        if x < 3:
            return wt.at[owner, x, pl.ds(part * half_m, half_m)]
        return wo_v.at[owner, pl.ds(pl.multiple_of(part * half_g, half_g), half_g)]

    def w_copy(source, target, stage, x, **device):
        return remote(source, target, w_send.at[stage, x], w_recv.at[stage, x], **device)

    w_far, w_near, w_local, w_over, w_pass, w_rest = [], [], [], [], [], []
    w_over_in, w_pass_in, w_rest_in = [], [], []
    for x in range(4):
        if x < 3:
            own, own_half = w_any.at[:, x], w_any.at[pl.ds(side * half_m, half_m), x]
        else:
            own = wo_any
            own_half = wo_any.at[pl.ds(pl.multiple_of(side * half_g, half_g), half_g)]
        w_far.append(w_copy(own_half, w_half(c, x, side), 0, x, head=far))
        w_near.append(w_copy(own, w_block(c, x), 1, x, head=near))
        w_local.append(pltpu.make_async_copy(own, w_block(c, x), local_sem.at[x]))
        ref = w_half(far, x, side)
        w_over.append(w_copy(ref, ref, 2, x, groups=across))
        w_pass.append(w_copy(ref, ref, 3, x, head=near))
        ref = w_half(far, x, across)
        w_over_in.append(w_copy(ref, ref, 2, x, groups=across))
        w_rest.append(w_copy(ref, ref, 4, x, head=near))
        ref = w_half(near_far, x, side)
        w_pass_in.append(w_copy(ref, ref, 3, x, head=near))
        ref = w_half(near_far, x, across)
        w_rest_in.append(w_copy(ref, ref, 4, x, head=near))

    def w_first(x):
        w_far[x].wait_recv()
        w_over[x].start()
        w_pass[x].start()

    def w_second(x):
        w_over_in[x].wait_recv()
        w_rest[x].start()

    def w_ready(x):
        w_local[x].wait()
        w_near[x].wait_recv()
        w_pass_in[x].wait_recv()
        w_rest_in[x].wait_recv()

    for x in (1, 2, 0, 3):
        w_far[x].start()
    loads[0].wait()
    route_copies = []
    for n in range(NC):
        loads[1 + n].wait()
        projected = dot(tile_v[...], embed_v[n]).astype(jnp.bfloat16)
        outgoing[n] = dot(pick, projected).astype(jnp.bfloat16).reshape(S, cap, cols)
        row = []
        for k in range(1, S):
            copy = remote(
                outgoing.at[n, seq_to[k]],
                arrived.at[n, s],
                route_send.at[n, k],
                route_recv.at[n, k],
                seq=seq_to[k],
            )
            copy.start()
            row.append(copy)
        route_copies.append(row)
        arrived[n, s] = outgoing[n, s]
    for x in (1, 2, 0, 3):
        w_local[x].start()
        w_near[x].start()

    def original(position):
        return (position % p3) * d3 + ((position // p3) % (d3 // d2)) * d2 + position // p2

    for copy in slot_copies:
        copy.wait_recv()
    slots = jnp.concatenate([slot_in[t][0:1, :] for t in range(S)], axis=1)
    landing = jnp.where(original(iota((R, S * cap), 0)) + 1 == slots, 1.0, 0.0).astype(jnp.bfloat16)
    back = jnp.where(original(iota((R, R), 1)) == iota((R, R), 0), 1.0, 0.0).astype(jnp.bfloat16)

    w_first(1)
    w_first(2)
    w_second(1)
    w_first(0)
    w_second(2)
    w_first(3)
    w_second(0)
    parts = []
    for n in range(NC):
        for copy in route_copies[n]:
            copy.wait_recv()
        parts.append(dot(landing, arrived[n].reshape(S * cap, cols)))
    embedded = jnp.concatenate(parts, axis=1)
    emb[...] = embedded.astype(jnp.bfloat16)
    normed = layer_norm(embedded, gain_ref[...])

    w_ready(1)
    w_ready(2)
    lane_head = (iota((p2, 2 * G), 1) % G) // E
    for g in range(SH):
        kv = dot_nt(normed, wt[g, 1:3].reshape(2 * G, D))
        kvs[g] = kv.astype(jnp.bfloat16)
        chosen = kv[0:p2]
        for m in range(1, M):
            chosen = jnp.where(lane_head == m, kv[m * p2 : (m + 1) * p2], chosen)
        chosen = chosen.astype(jnp.bfloat16)
        kv2[c, g] = chosen
        kx3[g] = chosen[g * p3 : (g + 1) * p3]
    kv2_far = remote(kv2.at[c], kv2.at[c], kv2_send.at[0], kv2_recv.at[0], head=far)
    kv2_near = remote(kv2.at[c], kv2.at[c], kv2_send.at[1], kv2_recv.at[1], head=near)
    kv2_relay = remote(kv2.at[far], kv2.at[far], kv2_send.at[2], kv2_recv.at[2], head=near)
    kv2_relay_in = remote(
        kv2.at[near_far], kv2.at[near_far], kv2_send.at[2], kv2_recv.at[2], head=near
    )
    kx3_copies = []
    for k in range(1, S):
        copy = remote(kx3, kv3.at[s, c], kx3_send.at[k], kx3_recv.at[k], seq=seq_to[k])
        copy.start()
        kx3_copies.append(copy)
    kv2_far.start()
    kv2_near.start()
    w_second(3)
    w_ready(0)
    for g in range(SH):
        qs[g] = dot_nt(normed, wt[g, 0].reshape(G, D)).astype(jnp.bfloat16)

    q_head = iota((R, G), 1) // E
    v_head = (iota((R, VW), 1) - lead + 2 * E) // E - 2

    def scale_one(g, carry):
        queries = qs[g]
        keys = kvs[g, :, 0:G]
        values = kvs[g, :, v_low : 2 * G]
        numer = jnp.zeros((R, VW), jnp.float32)
        peak = jnp.zeros((R, VW), jnp.float32)
        denom = jnp.ones((R, VW), jnp.float32)
        for m in range(M):
            mask = jnp.where(q_head == m, 1.0, 0.0).astype(jnp.bfloat16)
            scores = dot_nt(queries * mask, keys)
            row_max = jnp.max(scores, axis=-1, keepdims=True)
            expo = jnp.exp((scores - row_max) * scale)
            total = jnp.sum(expo, axis=-1, keepdims=True)
            head_out = dot(expo.astype(jnp.bfloat16), values)
            mine = v_head == m
            numer = jnp.where(mine, head_out, numer)
            peak = jnp.where(mine, row_max, peak)
            denom = jnp.where(mine, total, denom)
        num[g] = numer
        top[g] = peak
        den[g] = denom
        return carry

    lax.fori_loop(0, SH - 1, scale_one, 0)
    kv2_far.wait_recv()
    kv2_relay.start()
    kv3_far, kv3_near, kv3_relay, kv3_relay_in = [], [], [], []
    for k in range(1, S):
        kx3_copies[k - 1].wait_recv()
        block = kv3.at[seq_from[k], c]
        kv3_far.append(remote(block, block, kv3_send.at[0, k], kv3_recv.at[0, k], head=far))
        kv3_near.append(remote(block, block, kv3_send.at[1, k], kv3_recv.at[1, k], head=near))
        kv3_far[-1].start()
        kv3_near[-1].start()
        block = kv3.at[seq_from[k], far]
        kv3_relay.append(remote(block, block, kv3_send.at[2, k], kv3_recv.at[2, k], head=near))
        block = kv3.at[seq_from[k], near_far]
        kv3_relay_in.append(remote(block, block, kv3_send.at[2, k], kv3_recv.at[2, k], head=near))
    lax.fori_loop(SH - 1, SH, scale_one, 0)

    kv2_near.wait_recv()
    kv2_relay_in.wait_recv()

    def merge(g, rows, mine, row_max, total, head_out):
        old = top[g, rows, :]
        this = jnp.where(mine, row_max, LOWEST)
        peak = jnp.maximum(old, this)
        keep = jnp.exp((old - peak) * scale)
        add = jnp.where(mine, jnp.exp((this - peak) * scale), 0.0)
        top[g, rows, :] = peak
        num[g, rows, :] = num[g, rows, :] * keep + head_out * add
        den[g, rows, :] = den[g, rows, :] * keep + total * add

    q_diag = jnp.where(q_head == iota((R, G), 0) // p2, 1.0, 0.0).astype(jnp.bfloat16)
    v_diag = v_head == iota((R, VW), 0) // p2

    def scale_two(g, carry):
        keys = kv2[:, g, :, 0:G].reshape(H * p2, G)
        values = kv2[:, g, :, v_low : 2 * G].reshape(H * p2, VW)
        scores = dot_nt(qs[g] * q_diag, keys)
        row_max = jnp.max(scores, axis=-1, keepdims=True)
        expo = jnp.exp((scores - row_max) * scale)
        total = jnp.sum(expo, axis=-1, keepdims=True)
        head_out = dot(expo.astype(jnp.bfloat16), values)
        merge(g, pl.ds(0, R), v_diag, row_max, total, head_out)
        return carry

    lax.fori_loop(0, SH, scale_two, 0)
    for k in range(1, S):
        kv3_far[k - 1].wait_recv()
        kv3_relay[k - 1].start()
    for g in range(SH):
        for other in range(H):
            kv3[s, other, g] = kv2[other, g, g * p3 : (g + 1) * p3, :]
    residual = dot(back, emb[...])
    for k in range(1, S):
        kv3_near[k - 1].wait_recv()
        kv3_relay_in[k - 1].wait_recv()

    q_small = jnp.where(
        iota((M * p3, G), 1) // E == iota((M * p3, G), 0) // p3, 1.0, 0.0
    ).astype(jnp.bfloat16)

    def scale_three(g, carry):
        starts = [pl.multiple_of(m * p2 + g * p3, p3) for m in range(M)]
        queries = jnp.concatenate([qs[g, pl.ds(start, p3), :] for start in starts], axis=0)
        keys = kv3[:, :, g, :, 0:G].reshape(S * H * p3, G)
        values = kv3[:, :, g, :, v_low : 2 * G].reshape(S * H * p3, VW)
        scores = dot_nt(queries * q_small, keys)
        row_max = jnp.max(scores, axis=-1, keepdims=True)
        expo = jnp.exp((scores - row_max) * scale)
        total = jnp.sum(expo, axis=-1, keepdims=True)
        head_out = dot(expo.astype(jnp.bfloat16), values)
        for m in range(M):
            part = slice(m * p3, (m + 1) * p3)
            merge(
                g,
                pl.ds(starts[m], p3),
                (iota((p3, VW), 1) >= lead + m * E) & (iota((p3, VW), 1) < lead + (m + 1) * E),
                row_max[part],
                total[part],
                head_out[part],
            )
        return carry

    lax.fori_loop(0, SH, scale_three, 0)

    w_ready(3)
    mixed = residual
    for g in range(SH):
        attention = (num[g] / den[g]).astype(jnp.bfloat16)
        ordered = dot(back, attention)[:, lead:VW].astype(jnp.bfloat16)
        mixed = mixed + dot(ordered, wo_v[g])
    out_ref[...] = mixed.astype(jnp.bfloat16)

    sent = slot_copies + w_far + w_near + w_over + w_pass + w_rest + [kv2_far, kv2_near, kv2_relay] + kx3_copies
    sent += kv3_far + kv3_near + kv3_relay
    for row in route_copies:
        sent += row
    for copy in sent:
        copy.wait_send()


def fused(tile_rows, tile_route, embed_weight, norm_gain, qkv_weight, out_weight):
    S = lax.axis_size("seq")
    H = lax.axis_size("head")
    R, d_in = tile_rows.shape
    D = embed_weight.shape[1]
    M, E = qkv_weight.shape[1], qkv_weight.shape[3]
    G = M * E
    cap = 2 * R // S
    NC = D // 256
    SH = H
    d2, d3 = DILATIONS[1:]
    p2, p3 = R // d2, R // d3
    VW = 2 * G - G // 128 * 128
    bf, f32 = jnp.bfloat16, jnp.float32
    any_spec = pl.BlockSpec(memory_space=pl.ANY)
    vmem = pl.BlockSpec(memory_space=pltpu.VMEM)
    dma = pltpu.SemaphoreType.DMA
    return pl.pallas_call(
        functools.partial(layer_kernel, (S, H, R, D, NC, M, E, SH, d2, d3)),
        out_shape=jax.ShapeDtypeStruct((R, D), bf),
        in_specs=[any_spec, vmem, any_spec, vmem, any_spec, any_spec],
        out_specs=vmem,
        scratch_shapes=[
            pltpu.VMEM((R, d_in), bf),
            pltpu.VMEM((NC, d_in, 256), bf),
            pltpu.VMEM((H, 3, M, E, D), bf),
            pltpu.VMEM((H, G, D), bf),
            pltpu.VMEM((NC, S, cap, 256), bf),
            pltpu.VMEM((NC, S, cap, 256), bf),
            pltpu.VMEM((S, 8, cap), jnp.int32),
            pltpu.VMEM((S, 8, cap), jnp.int32),
            pltpu.VMEM((R, D), bf),
            pltpu.VMEM((SH, R, G), bf),
            pltpu.VMEM((SH, R, 2 * G), bf),
            pltpu.VMEM((H, SH, p2, 2 * G), bf),
            pltpu.VMEM((SH, p3, 2 * G), bf),
            pltpu.VMEM((S, H, SH, p3, 2 * G), bf),
            pltpu.VMEM((SH, R, VW), f32),
            pltpu.VMEM((SH, R, VW), f32),
            pltpu.VMEM((SH, R, VW), f32),
            dma((1 + NC,)),
            dma((4,)),
            dma((5, 4)),
            dma((5, 4)),
            dma((NC, S)),
            dma((NC, S)),
            dma((S,)),
            dma((S,)),
            dma((3,)),
            dma((3,)),
            dma((S,)),
            dma((S,)),
            dma((3, S)),
            dma((3, S)),
        ],
        compiler_params=pltpu.CompilerParams(
            collective_id=0, has_side_effects=True, vmem_limit_bytes=56 * 1024 * 1024
        ),
    )(
        tile_rows,
        tile_route.T,
        embed_weight,
        norm_gain.reshape(1, D),
        qkv_weight.transpose(1, 2, 3, 0),
        out_weight,
    )


def fits(mesh):
    def check(tile_rows, embed_weight, qkv_weight):
        S, H = mesh.shape["seq"], mesh.shape["head"]
        rows = tile_rows.shape[0] // mesh.size
        heads = qkv_weight.shape[1] // H
        d2, d3 = DILATIONS[1:]
        return (
            H == 4
            and mesh.shape["groups"] == 2
            and heads == d2
            and heads * H == d3
            and FRACTIONS[0] == S * H
            and FRACTIONS[1] == S
            and FRACTIONS[2] == 1
            and rows % (16 * d3) == 0
            and rows <= 256
            and embed_weight.shape[1] % 256 == 0
            and embed_weight.shape[1] // 256 >= 3
        )

    return check


def solution(mesh):
    check = fits(mesh)

    def program(tile_rows, tile_route, embed_weight, norm_gain, qkv_weight, out_weight):
        body = fused if check(tile_rows, embed_weight, qkv_weight) else local
        return jax.shard_map(
            body,
            mesh=mesh,
            in_specs=(
                P(("groups", "seq", "head"), None),
                P(("groups", "seq", "head"), None),
                P(),
                P(),
                P(None, "head", None, None),
                P("head", None),
            ),
            out_specs=P(("groups", "seq", "head"), None),
            check_vma=False,
        )(tile_rows, tile_route, embed_weight, norm_gain, qkv_weight, out_weight)

    return program
```

```python
import functools

import jax
import jax.numpy as jnp
from jax import lax
from jax.experimental import pallas as pl
from jax.experimental.pallas import tpu as pltpu
from jax.sharding import PartitionSpec as P

EPSILON = 1e-05
DILATIONS = (1, 4, 16)
FRACTIONS = (16, 4, 1)


def from_partner(block, axis, apart):
    count = lax.axis_size(axis)
    route = []
    for low in range(count):
        high = low | 1 << apart
        if high != low and high < count:
            route += [(low, high), (high, low)]
    return lax.ppermute(block, axis, route)


def layer_norm(rows, gain):
    row_mean = jnp.mean(rows, axis=-1, keepdims=True)
    centered = rows - row_mean
    row_var = jnp.mean(centered * centered, axis=-1, keepdims=True)
    return (centered * lax.rsqrt(row_var + EPSILON) * gain).astype(jnp.bfloat16)


def attend_block(queries, key_rows, values):
    score_scale = queries.shape[-1] ** (-0.5)
    scores = jnp.dot(queries, key_rows.T, preferred_element_type=jnp.float32) * score_scale
    row_max = jnp.max(scores, axis=-1)
    expo = jnp.exp(scores - row_max[:, None])
    denominator = jnp.sum(expo, axis=-1)
    weights = (expo / denominator[:, None]).astype(jnp.bfloat16)
    head_out = jnp.dot(weights, values, preferred_element_type=jnp.float32)
    return (head_out, row_max + jnp.log(denominator))


def attend(queries, key_rows, values):
    count = queries.shape[0]
    if count > 512 and count % 512 == 0:
        blocks = queries.reshape(count // 512, 512, queries.shape[1])
        head_out, log_total = lax.map(
            lambda block_in: attend_block(block_in, key_rows, values), blocks
        )
        return (head_out.reshape(count, -1), log_total.reshape(count))
    return attend_block(queries, key_rows, values)


def expand_rows(head_out, log_total, offset, dilation):
    count = head_out.shape[0]
    pick_mask = jnp.arange(dilation, dtype=jnp.int32) == offset
    full_out = jnp.where(pick_mask[None, :, None], head_out[:, None, :], 0.0).reshape(
        count * dilation, -1
    )
    full_total = jnp.where(pick_mask[None, :], log_total[:, None], -1e30).reshape(count * dilation)
    return (full_out, full_total)


def merge_scales(outputs, totals):
    row_max = jnp.maximum(jnp.maximum(totals[0], totals[1]), totals[2])
    numer = jnp.zeros_like(outputs[0])
    denom = jnp.zeros_like(totals[0])
    for full_out, full_total in zip(outputs, totals):
        factor = jnp.exp(full_total - row_max)
        numer = numer + factor[:, None] * full_out
        denom = denom + factor
    return numer / denom[:, None]


def collect_segment(flat_rows, levels, seq_index):
    for level in range(levels):
        partner = from_partner(flat_rows, "seq", level)
        upper_half = seq_index >> level & 1 == 1
        lower_rows = jnp.where(upper_half, partner, flat_rows)
        upper_rows = jnp.where(upper_half, flat_rows, partner)
        flat_rows = jnp.concatenate([lower_rows, upper_rows], axis=0)
    return flat_rows


def local(tile_rows, tile_route, embed_weight, norm_gain, qkv_weight, out_weight):
    seq_count = lax.axis_size("seq")
    seq_index = lax.axis_index("seq")
    in_rows = tile_rows.shape[0]
    width = embed_weight.shape[1]
    capacity = 2 * in_rows // seq_count
    projected = jnp.dot(tile_rows, embed_weight, preferred_element_type=jnp.float32).astype(
        jnp.bfloat16
    )
    dest_seq = tile_route[:, 0]
    slot_index = tile_route[:, 1]
    owner_hits = (dest_seq[:, None] == jnp.arange(seq_count, dtype=jnp.int32)[None, :]).astype(
        jnp.int32
    )
    earlier = jnp.cumsum(owner_hits, axis=0) - owner_hits
    owner_rank = jnp.sum(earlier * owner_hits, axis=1)
    buffer_place = dest_seq * capacity + owner_rank
    send_pick = jnp.arange(seq_count * capacity, dtype=jnp.int32)[:, None] == buffer_place[None, :]
    outgoing = jnp.dot(
        send_pick.astype(jnp.bfloat16), projected, preferred_element_type=jnp.float32
    ).astype(jnp.bfloat16)
    outgoing_slot = jnp.sum(jnp.where(send_pick, slot_index[None, :] + 1, 0), axis=1)
    arrived, arrived_slot = (
        lax.all_to_all(
            outgoing.reshape(seq_count, capacity, width),
            "seq",
            split_axis=0,
            concat_axis=0,
            tiled=True,
        ),
        lax.all_to_all(
            outgoing_slot.reshape(seq_count, capacity),
            "seq",
            split_axis=0,
            concat_axis=0,
            tiled=True,
        ),
    )
    landing = jnp.arange(in_rows, dtype=jnp.int32)[:, None] + 1 == arrived_slot.reshape(-1)[None, :]
    embedded = jnp.dot(
        landing.astype(jnp.bfloat16), arrived.reshape(-1, width), preferred_element_type=jnp.float32
    )
    normed = layer_norm(embedded, norm_gain)
    heads_here = qkv_weight.shape[1]
    head_dim = qkv_weight.shape[3]
    weight_flat = qkv_weight.reshape(width, -1)
    qkv = jnp.dot(
        lax.all_gather(normed, "head", axis=0, tiled=True),
        weight_flat,
        preferred_element_type=jnp.float32,
    ).astype(jnp.bfloat16)
    rows_here = qkv.shape[0]
    qkv = qkv.reshape(rows_here, heads_here, 3, head_dim)
    first_head = lax.axis_index("head") * heads_here
    total_rows = rows_here * seq_count
    outputs = [[] for member in range(heads_here)]
    totals = [[] for member in range(heads_here)]
    for fraction, dilation in zip(FRACTIONS, DILATIONS):
        segment = total_rows // fraction
        per_segment = segment // dilation
        count = rows_here // dilation
        shaped = qkv.reshape(count, dilation, heads_here, 3, head_dim)
        offsets = []
        chosen = []
        for member in range(heads_here):
            offset = (first_head + member) % dilation
            offsets.append(offset)
            chosen.append(
                lax.dynamic_index_in_dim(shaped[:, :, member], offset, axis=1, keepdims=False)
            )
        chosen = jnp.stack(chosen, axis=1)
        queries = chosen[:, :, 0]
        pairs = chosen[:, :, 1:]
        if segment > rows_here:
            levels = (segment // rows_here).bit_length() - 1
            flat_rows = collect_segment(pairs.reshape(count, -1), levels, seq_index)
            pairs = flat_rows.reshape(per_segment, heads_here, 2, head_dim)
            groups = 1
        else:
            groups = rows_here // segment
        grouped_queries = queries.reshape(groups, count // groups, heads_here, head_dim)
        grouped_pairs = pairs.reshape(groups, per_segment, heads_here, 2, head_dim)
        for member in range(heads_here):
            head_out, log_total = lax.map(
                lambda block_in: attend(block_in[0], block_in[1][:, 0], block_in[1][:, 1]),
                (grouped_queries[:, :, member], grouped_pairs[:, :, member]),
            )
            full_out, full_total = expand_rows(
                head_out.reshape(count, head_dim),
                log_total.reshape(count),
                offsets[member],
                dilation,
            )
            outputs[member].append(full_out)
            totals[member].append(full_total)
    merged = [
        merge_scales(outputs[member], totals[member]).astype(jnp.bfloat16)
        for member in range(heads_here)
    ]
    attention = jnp.stack(merged, axis=1).reshape(rows_here, heads_here * head_dim)
    regrouped = lax.all_to_all(attention, "head", split_axis=0, concat_axis=1, tiled=True)
    branch = jnp.dot(
        regrouped,
        lax.all_gather(out_weight, "head", axis=0, tiled=True),
        preferred_element_type=jnp.float32,
    )
    return (embedded + branch).astype(jnp.bfloat16)


MESH = pl.DeviceIdType.MESH
LOWEST = -1e30


def dot_nt(a, b):
    return lax.dot_general(a, b, (((1,), (1,)), ((), ())), preferred_element_type=jnp.float32)


def dot(a, b):
    return jnp.dot(a, b, preferred_element_type=jnp.float32)


def iota(shape, dim):
    return lax.broadcasted_iota(jnp.int32, shape, dim)


def layer_kernel(
    dims,
    tile_any,
    route_ref,
    embed_any,
    gain_ref,
    w_any,
    wo_any,
    out_ref,
    tile_v,
    embed_v,
    wt,
    wo_v,
    outgoing,
    arrived,
    slot_out,
    slot_in,
    emb,
    qs,
    kvs,
    kv2,
    kx3,
    kv3,
    num,
    top,
    den,
    load_sem,
    local_sem,
    w_send,
    w_recv,
    route_send,
    route_recv,
    slot_send,
    slot_recv,
    kv2_send,
    kv2_recv,
    kx3_send,
    kx3_recv,
    kv3_send,
    kv3_recv,
):
    S, H, R, D, NC, M, E, SH, d2, d3 = dims
    cap = arrived.shape[2]
    cols = arrived.shape[3]
    G = M * E
    p2 = R // d2
    p3 = R // d3
    v_low = G // 128 * 128
    VW = 2 * G - v_low
    lead = G - v_low
    scale = E ** (-0.5)
    s = lax.axis_index("seq")
    c = lax.axis_index("head")
    side = lax.axis_index("groups")
    across = 1 - side
    near = c + 1 - 2 * (c % 2)
    far = (c + 2) % H
    near_far = (near + 2) % H
    seq_to = [(s + k) % S for k in range(S)]
    seq_from = [(s + S - k) % S for k in range(S)]

    loads = [pltpu.make_async_copy(tile_any, tile_v, load_sem.at[0])]
    for n in range(NC):
        loads.append(
            pltpu.make_async_copy(
                embed_any.at[:, pl.ds(n * cols, cols)], embed_v.at[n], load_sem.at[1 + n]
            )
        )
    for copy in loads:
        copy.start()

    barrier = pltpu.get_barrier_semaphore()
    for k in range(1, S):
        pl.semaphore_signal(barrier, inc=1, device_id={"seq": seq_to[k]}, device_id_type=MESH)
    for peer in (near, far):
        pl.semaphore_signal(barrier, inc=1, device_id={"head": peer}, device_id_type=MESH)
    pl.semaphore_signal(barrier, inc=1, device_id={"groups": across}, device_id_type=MESH)

    dest = route_ref[0:1, :]
    slot = route_ref[1:2, :]
    sub = max(8, S)
    hits = iota((sub, R), 0) == dest
    hits_f = jnp.where(hits, 1.0, 0.0)
    below = jnp.where(iota((R, R), 0) < iota((R, R), 1), 1.0, 0.0).astype(jnp.bfloat16)
    earlier = dot(hits_f.astype(jnp.bfloat16), below)
    rank = jnp.sum(earlier * hits_f, axis=0, keepdims=True).astype(jnp.int32)
    place = dest * cap + rank
    pick = jnp.where(iota((S * cap, R), 0) == place, 1.0, 0.0).astype(jnp.bfloat16)
    slot_f = jnp.broadcast_to((slot + 1).astype(jnp.float32), (8, R)).astype(jnp.bfloat16)
    slot_rows = dot_nt(slot_f, pick).astype(jnp.int32)
    for t in range(S):
        slot_out[t] = slot_rows[:, t * cap : (t + 1) * cap]

    pl.semaphore_wait(barrier, S - 1 + 3)

    def remote(src, dst, send, recv, **device):
        copy = pltpu.make_async_remote_copy(
            src_ref=src,
            dst_ref=dst,
            send_sem=send,
            recv_sem=recv,
            device_id=device,
            device_id_type=MESH,
        )
        return copy

    slot_copies = []
    for k in range(1, S):
        copy = remote(
            slot_out.at[seq_to[k]], slot_in.at[s], slot_send.at[k], slot_recv.at[k], seq=seq_to[k]
        )
        copy.start()
        slot_copies.append(copy)
    slot_in[s] = slot_out[s]

    half_m, half_g = M // 2, G // 2

    def w_block(owner, x):
        return wt.at[owner, x] if x < 3 else wo_v.at[owner]

    def w_half(owner, x, part):
        if x < 3:
            return wt.at[owner, x, pl.ds(part * half_m, half_m)]
        return wo_v.at[owner, pl.ds(pl.multiple_of(part * half_g, half_g), half_g)]

    def w_copy(source, target, stage, x, **device):
        return remote(source, target, w_send.at[stage, x], w_recv.at[stage, x], **device)

    w_far, w_near, w_local, w_over, w_pass, w_rest = [], [], [], [], [], []
    w_over_in, w_pass_in, w_rest_in = [], [], []
    for x in range(4):
        if x < 3:
            own, own_half = w_any.at[:, x], w_any.at[pl.ds(side * half_m, half_m), x]
        else:
            own = wo_any
            own_half = wo_any.at[pl.ds(pl.multiple_of(side * half_g, half_g), half_g)]
        w_far.append(w_copy(own_half, w_half(c, x, side), 0, x, head=far))
        w_near.append(w_copy(own, w_block(c, x), 1, x, head=near))
        w_local.append(pltpu.make_async_copy(own, w_block(c, x), local_sem.at[x]))
        ref = w_half(far, x, side)
        w_over.append(w_copy(ref, ref, 2, x, groups=across))
        w_pass.append(w_copy(ref, ref, 3, x, head=near))
        ref = w_half(far, x, across)
        w_over_in.append(w_copy(ref, ref, 2, x, groups=across))
        w_rest.append(w_copy(ref, ref, 4, x, head=near))
        ref = w_half(near_far, x, side)
        w_pass_in.append(w_copy(ref, ref, 3, x, head=near))
        ref = w_half(near_far, x, across)
        w_rest_in.append(w_copy(ref, ref, 4, x, head=near))

    def w_first(x):
        w_far[x].wait_recv()
        w_over[x].start()
        w_pass[x].start()

    def w_second(x):
        w_over_in[x].wait_recv()
        w_rest[x].start()

    def w_ready(x):
        w_local[x].wait()
        w_near[x].wait_recv()
        w_pass_in[x].wait_recv()
        w_rest_in[x].wait_recv()

    loads[0].wait()
    route_copies = []
    for n in range(NC):
        loads[1 + n].wait()
        projected = dot(tile_v[...], embed_v[n]).astype(jnp.bfloat16)
        outgoing[n] = dot(pick, projected).astype(jnp.bfloat16).reshape(S, cap, cols)
        row = []
        for k in range(1, S):
            copy = remote(
                outgoing.at[n, seq_to[k]],
                arrived.at[n, s],
                route_send.at[n, k],
                route_recv.at[n, k],
                seq=seq_to[k],
            )
            copy.start()
            row.append(copy)
        route_copies.append(row)
        if n == 0:
            for x in (1, 2, 0, 3):
                w_far[x].start()
        arrived[n, s] = outgoing[n, s]
    for x in (1, 2, 0, 3):
        w_local[x].start()
        w_near[x].start()

    def original(position):
        return (position % p3) * d3 + ((position // p3) % (d3 // d2)) * d2 + position // p2

    for copy in slot_copies:
        copy.wait_recv()
    slots = jnp.concatenate([slot_in[t][0:1, :] for t in range(S)], axis=1)
    landing = jnp.where(original(iota((R, S * cap), 0)) + 1 == slots, 1.0, 0.0).astype(jnp.bfloat16)
    back = jnp.where(original(iota((R, R), 1)) == iota((R, R), 0), 1.0, 0.0).astype(jnp.bfloat16)

    w_first(1)
    w_first(2)
    w_second(1)
    w_first(0)
    w_second(2)
    w_second(0)
    parts = []
    for n in range(NC):
        for copy in route_copies[n]:
            copy.wait_recv()
        parts.append(dot(landing, arrived[n].reshape(S * cap, cols)))
    embedded = jnp.concatenate(parts, axis=1)
    emb[...] = embedded.astype(jnp.bfloat16)
    normed = layer_norm(embedded, gain_ref[...].reshape(1, D))

    w_ready(1)
    w_ready(2)
    lane_head = (iota((p2, 2 * G), 1) % G) // E
    for g in range(SH):
        kv = dot_nt(normed, wt[g, 1:3].reshape(2 * G, D))
        kvs[g] = kv.astype(jnp.bfloat16)
        chosen = kv[0:p2]
        for m in range(1, M):
            chosen = jnp.where(lane_head == m, kv[m * p2 : (m + 1) * p2], chosen)
        chosen = chosen.astype(jnp.bfloat16)
        kv2[c, g] = chosen
        kx3[g] = chosen[g * p3 : (g + 1) * p3]
    kv2_far = remote(kv2.at[c], kv2.at[c], kv2_send.at[0], kv2_recv.at[0], head=far)
    kv2_near = remote(kv2.at[c], kv2.at[c], kv2_send.at[1], kv2_recv.at[1], head=near)
    kv2_relay = remote(kv2.at[far], kv2.at[far], kv2_send.at[2], kv2_recv.at[2], head=near)
    kv2_relay_in = remote(
        kv2.at[near_far], kv2.at[near_far], kv2_send.at[2], kv2_recv.at[2], head=near
    )
    kx3_copies = []
    for k in range(1, S):
        copy = remote(kx3, kv3.at[s, c], kx3_send.at[k], kx3_recv.at[k], seq=seq_to[k])
        copy.start()
        kx3_copies.append(copy)
    kv2_far.start()
    kv2_near.start()
    w_first(3)
    w_ready(0)
    for g in range(SH):
        qs[g] = dot_nt(normed, wt[g, 0].reshape(G, D)).astype(jnp.bfloat16)

    q_head = iota((R, G), 1) // E
    v_head = (iota((R, VW), 1) - lead + 2 * E) // E - 2

    def scale_one(g, carry):
        queries = qs[g]
        keys = kvs[g, :, 0:G]
        values = kvs[g, :, v_low : 2 * G]
        numer = jnp.zeros((R, VW), jnp.float32)
        peak = jnp.zeros((R, VW), jnp.float32)
        denom = jnp.ones((R, VW), jnp.float32)
        for m in range(M):
            mask = jnp.where(q_head == m, 1.0, 0.0).astype(jnp.bfloat16)
            scores = dot_nt(queries * mask, keys)
            row_max = jnp.max(scores, axis=-1, keepdims=True)
            expo = jnp.exp((scores - row_max) * scale)
            total = jnp.sum(expo, axis=-1, keepdims=True)
            head_out = dot(expo.astype(jnp.bfloat16), values)
            mine = v_head == m
            numer = jnp.where(mine, head_out, numer)
            peak = jnp.where(mine, row_max, peak)
            denom = jnp.where(mine, total, denom)
        num[g] = numer
        top[g] = peak
        den[g] = denom
        return carry

    lax.fori_loop(0, SH - 1, scale_one, 0)
    w_second(3)
    kv2_far.wait_recv()
    kv2_relay.start()
    kv3_far, kv3_near, kv3_relay, kv3_relay_in = [], [], [], []
    for k in range(1, S):
        kx3_copies[k - 1].wait_recv()
        block = kv3.at[seq_from[k], c]
        kv3_far.append(remote(block, block, kv3_send.at[0, k], kv3_recv.at[0, k], head=far))
        kv3_near.append(remote(block, block, kv3_send.at[1, k], kv3_recv.at[1, k], head=near))
        kv3_far[-1].start()
        kv3_near[-1].start()
        block = kv3.at[seq_from[k], far]
        kv3_relay.append(remote(block, block, kv3_send.at[2, k], kv3_recv.at[2, k], head=near))
        block = kv3.at[seq_from[k], near_far]
        kv3_relay_in.append(remote(block, block, kv3_send.at[2, k], kv3_recv.at[2, k], head=near))
    lax.fori_loop(SH - 1, SH, scale_one, 0)

    kv2_near.wait_recv()
    kv2_relay_in.wait_recv()

    def merge(g, rows, mine, row_max, total, head_out):
        old = top[g, rows, :]
        this = jnp.where(mine, row_max, LOWEST)
        peak = jnp.maximum(old, this)
        keep = jnp.exp((old - peak) * scale)
        add = jnp.where(mine, jnp.exp((this - peak) * scale), 0.0)
        top[g, rows, :] = peak
        num[g, rows, :] = num[g, rows, :] * keep + head_out * add
        den[g, rows, :] = den[g, rows, :] * keep + total * add

    q_diag = jnp.where(q_head == iota((R, G), 0) // p2, 1.0, 0.0).astype(jnp.bfloat16)
    v_diag = v_head == iota((R, VW), 0) // p2

    def scale_two(g, carry):
        keys = kv2[:, g, :, 0:G].reshape(H * p2, G)
        values = kv2[:, g, :, v_low : 2 * G].reshape(H * p2, VW)
        scores = dot_nt(qs[g] * q_diag, keys)
        row_max = jnp.max(scores, axis=-1, keepdims=True)
        expo = jnp.exp((scores - row_max) * scale)
        total = jnp.sum(expo, axis=-1, keepdims=True)
        head_out = dot(expo.astype(jnp.bfloat16), values)
        merge(g, pl.ds(0, R), v_diag, row_max, total, head_out)
        return carry

    lax.fori_loop(0, SH, scale_two, 0)
    for k in range(1, S):
        kv3_far[k - 1].wait_recv()
        kv3_relay[k - 1].start()
    for g in range(SH):
        for other in range(H):
            kv3[s, other, g] = kv2[other, g, g * p3 : (g + 1) * p3, :]
    residual = dot(back, emb[...])
    for k in range(1, S):
        kv3_near[k - 1].wait_recv()
        kv3_relay_in[k - 1].wait_recv()

    q_small = jnp.where(
        iota((M * p3, G), 1) // E == iota((M * p3, G), 0) // p3, 1.0, 0.0
    ).astype(jnp.bfloat16)

    def scale_three(g, carry):
        starts = [pl.multiple_of(m * p2 + g * p3, p3) for m in range(M)]
        queries = jnp.concatenate([qs[g, pl.ds(start, p3), :] for start in starts], axis=0)
        keys = kv3[:, :, g, :, 0:G].reshape(S * H * p3, G)
        values = kv3[:, :, g, :, v_low : 2 * G].reshape(S * H * p3, VW)
        scores = dot_nt(queries * q_small, keys)
        row_max = jnp.max(scores, axis=-1, keepdims=True)
        expo = jnp.exp((scores - row_max) * scale)
        total = jnp.sum(expo, axis=-1, keepdims=True)
        head_out = dot(expo.astype(jnp.bfloat16), values)
        for m in range(M):
            part = slice(m * p3, (m + 1) * p3)
            merge(
                g,
                pl.ds(starts[m], p3),
                (iota((p3, VW), 1) >= lead + m * E) & (iota((p3, VW), 1) < lead + (m + 1) * E),
                row_max[part],
                total[part],
                head_out[part],
            )
        return carry

    lax.fori_loop(0, SH, scale_three, 0)

    w_ready(3)
    mixed = residual
    for g in range(SH):
        attention = (num[g] / den[g]).astype(jnp.bfloat16)
        ordered = dot(back, attention)[:, lead:VW].astype(jnp.bfloat16)
        mixed = mixed + dot(ordered, wo_v[g])
    out_ref[...] = mixed.astype(jnp.bfloat16)

    sent = slot_copies + w_far + w_near + w_over + w_pass + w_rest + [kv2_far, kv2_near, kv2_relay] + kx3_copies
    sent += kv3_far + kv3_near + kv3_relay
    for row in route_copies:
        sent += row
    for copy in sent:
        copy.wait_send()


def fused(tile_rows, tile_route, embed_weight, norm_gain, qkv_weight, out_weight):
    S = lax.axis_size("seq")
    H = lax.axis_size("head")
    R, d_in = tile_rows.shape
    D = embed_weight.shape[1]
    M, E = qkv_weight.shape[1], qkv_weight.shape[3]
    G = M * E
    cap = 2 * R // S
    NC = D // 256
    SH = H
    d2, d3 = DILATIONS[1:]
    p2, p3 = R // d2, R // d3
    VW = 2 * G - G // 128 * 128
    bf, f32 = jnp.bfloat16, jnp.float32
    any_spec = pl.BlockSpec(memory_space=pl.ANY)
    vmem = pl.BlockSpec(memory_space=pltpu.VMEM)
    dma = pltpu.SemaphoreType.DMA
    return pl.pallas_call(
        functools.partial(layer_kernel, (S, H, R, D, NC, M, E, SH, d2, d3)),
        out_shape=jax.ShapeDtypeStruct((R, D), bf),
        in_specs=[any_spec, vmem, any_spec, vmem, any_spec, any_spec],
        out_specs=vmem,
        scratch_shapes=[
            pltpu.VMEM((R, d_in), bf),
            pltpu.VMEM((NC, d_in, 256), bf),
            pltpu.VMEM((H, 3, M, E, D), bf),
            pltpu.VMEM((H, G, D), bf),
            pltpu.VMEM((NC, S, cap, 256), bf),
            pltpu.VMEM((NC, S, cap, 256), bf),
            pltpu.VMEM((S, 8, cap), jnp.int32),
            pltpu.VMEM((S, 8, cap), jnp.int32),
            pltpu.VMEM((R, D), bf),
            pltpu.VMEM((SH, R, G), bf),
            pltpu.VMEM((SH, R, 2 * G), bf),
            pltpu.VMEM((H, SH, p2, 2 * G), bf),
            pltpu.VMEM((SH, p3, 2 * G), bf),
            pltpu.VMEM((S, H, SH, p3, 2 * G), bf),
            pltpu.VMEM((SH, R, VW), f32),
            pltpu.VMEM((SH, R, VW), f32),
            pltpu.VMEM((SH, R, VW), f32),
            dma((1 + NC,)),
            dma((4,)),
            dma((5, 4)),
            dma((5, 4)),
            dma((NC, S)),
            dma((NC, S)),
            dma((S,)),
            dma((S,)),
            dma((3,)),
            dma((3,)),
            dma((S,)),
            dma((S,)),
            dma((3, S)),
            dma((3, S)),
        ],
        compiler_params=pltpu.CompilerParams(
            collective_id=0, has_side_effects=True, vmem_limit_bytes=56 * 1024 * 1024
        ),
    )(
        tile_rows,
        tile_route.T,
        embed_weight,
        norm_gain,
        qkv_weight.transpose(1, 2, 3, 0),
        out_weight,
    )


def fits(mesh):
    def check(tile_rows, embed_weight, qkv_weight):
        S, H = mesh.shape["seq"], mesh.shape["head"]
        rows = tile_rows.shape[0] // mesh.size
        heads = qkv_weight.shape[1] // H
        d2, d3 = DILATIONS[1:]
        return (
            H == 4
            and mesh.shape["groups"] == 2
            and heads == d2
            and heads * H == d3
            and FRACTIONS[0] == S * H
            and FRACTIONS[1] == S
            and FRACTIONS[2] == 1
            and rows % (16 * d3) == 0
            and rows <= 256
            and embed_weight.shape[1] % 256 == 0
            and embed_weight.shape[1] // 256 >= 3
        )

    return check


def solution(mesh):
    check = fits(mesh)

    def program(tile_rows, tile_route, embed_weight, norm_gain, qkv_weight, out_weight):
        body = fused if check(tile_rows, embed_weight, qkv_weight) else local
        return jax.shard_map(
            body,
            mesh=mesh,
            in_specs=(
                P(("groups", "seq", "head"), None),
                P(("groups", "seq", "head"), None),
                P(),
                P(),
                P(None, "head", None, None),
                P("head", None),
            ),
            out_specs=P(("groups", "seq", "head"), None),
            check_vma=False,
        )(tile_rows, tile_route, embed_weight, norm_gain, qkv_weight, out_weight)

    return program
```

```python
import functools

import jax
import jax.numpy as jnp
from jax import lax
from jax.experimental import pallas as pl
from jax.experimental.pallas import tpu as pltpu
from jax.sharding import PartitionSpec as P

EPSILON = 1e-05
DILATIONS = (1, 4, 16)
FRACTIONS = (16, 4, 1)


def from_partner(block, axis, apart):
    count = lax.axis_size(axis)
    route = []
    for low in range(count):
        high = low | 1 << apart
        if high != low and high < count:
            route += [(low, high), (high, low)]
    return lax.ppermute(block, axis, route)


def layer_norm(rows, gain):
    row_mean = jnp.mean(rows, axis=-1, keepdims=True)
    centered = rows - row_mean
    row_var = jnp.mean(centered * centered, axis=-1, keepdims=True)
    return (centered * lax.rsqrt(row_var + EPSILON) * gain).astype(jnp.bfloat16)


def attend_block(queries, key_rows, values):
    score_scale = queries.shape[-1] ** (-0.5)
    scores = jnp.dot(queries, key_rows.T, preferred_element_type=jnp.float32) * score_scale
    row_max = jnp.max(scores, axis=-1)
    expo = jnp.exp(scores - row_max[:, None])
    denominator = jnp.sum(expo, axis=-1)
    weights = (expo / denominator[:, None]).astype(jnp.bfloat16)
    head_out = jnp.dot(weights, values, preferred_element_type=jnp.float32)
    return (head_out, row_max + jnp.log(denominator))


def attend(queries, key_rows, values):
    count = queries.shape[0]
    if count > 512 and count % 512 == 0:
        blocks = queries.reshape(count // 512, 512, queries.shape[1])
        head_out, log_total = lax.map(
            lambda block_in: attend_block(block_in, key_rows, values), blocks
        )
        return (head_out.reshape(count, -1), log_total.reshape(count))
    return attend_block(queries, key_rows, values)


def expand_rows(head_out, log_total, offset, dilation):
    count = head_out.shape[0]
    pick_mask = jnp.arange(dilation, dtype=jnp.int32) == offset
    full_out = jnp.where(pick_mask[None, :, None], head_out[:, None, :], 0.0).reshape(
        count * dilation, -1
    )
    full_total = jnp.where(pick_mask[None, :], log_total[:, None], -1e30).reshape(count * dilation)
    return (full_out, full_total)


def merge_scales(outputs, totals):
    row_max = jnp.maximum(jnp.maximum(totals[0], totals[1]), totals[2])
    numer = jnp.zeros_like(outputs[0])
    denom = jnp.zeros_like(totals[0])
    for full_out, full_total in zip(outputs, totals):
        factor = jnp.exp(full_total - row_max)
        numer = numer + factor[:, None] * full_out
        denom = denom + factor
    return numer / denom[:, None]


def collect_segment(flat_rows, levels, seq_index):
    for level in range(levels):
        partner = from_partner(flat_rows, "seq", level)
        upper_half = seq_index >> level & 1 == 1
        lower_rows = jnp.where(upper_half, partner, flat_rows)
        upper_rows = jnp.where(upper_half, flat_rows, partner)
        flat_rows = jnp.concatenate([lower_rows, upper_rows], axis=0)
    return flat_rows


def local(tile_rows, tile_route, embed_weight, norm_gain, qkv_weight, out_weight):
    seq_count = lax.axis_size("seq")
    seq_index = lax.axis_index("seq")
    in_rows = tile_rows.shape[0]
    width = embed_weight.shape[1]
    capacity = 2 * in_rows // seq_count
    projected = jnp.dot(tile_rows, embed_weight, preferred_element_type=jnp.float32).astype(
        jnp.bfloat16
    )
    dest_seq = tile_route[:, 0]
    slot_index = tile_route[:, 1]
    owner_hits = (dest_seq[:, None] == jnp.arange(seq_count, dtype=jnp.int32)[None, :]).astype(
        jnp.int32
    )
    earlier = jnp.cumsum(owner_hits, axis=0) - owner_hits
    owner_rank = jnp.sum(earlier * owner_hits, axis=1)
    buffer_place = dest_seq * capacity + owner_rank
    send_pick = jnp.arange(seq_count * capacity, dtype=jnp.int32)[:, None] == buffer_place[None, :]
    outgoing = jnp.dot(
        send_pick.astype(jnp.bfloat16), projected, preferred_element_type=jnp.float32
    ).astype(jnp.bfloat16)
    outgoing_slot = jnp.sum(jnp.where(send_pick, slot_index[None, :] + 1, 0), axis=1)
    arrived, arrived_slot = (
        lax.all_to_all(
            outgoing.reshape(seq_count, capacity, width),
            "seq",
            split_axis=0,
            concat_axis=0,
            tiled=True,
        ),
        lax.all_to_all(
            outgoing_slot.reshape(seq_count, capacity),
            "seq",
            split_axis=0,
            concat_axis=0,
            tiled=True,
        ),
    )
    landing = jnp.arange(in_rows, dtype=jnp.int32)[:, None] + 1 == arrived_slot.reshape(-1)[None, :]
    embedded = jnp.dot(
        landing.astype(jnp.bfloat16), arrived.reshape(-1, width), preferred_element_type=jnp.float32
    )
    normed = layer_norm(embedded, norm_gain)
    heads_here = qkv_weight.shape[1]
    head_dim = qkv_weight.shape[3]
    weight_flat = qkv_weight.reshape(width, -1)
    qkv = jnp.dot(
        lax.all_gather(normed, "head", axis=0, tiled=True),
        weight_flat,
        preferred_element_type=jnp.float32,
    ).astype(jnp.bfloat16)
    rows_here = qkv.shape[0]
    qkv = qkv.reshape(rows_here, heads_here, 3, head_dim)
    first_head = lax.axis_index("head") * heads_here
    total_rows = rows_here * seq_count
    outputs = [[] for member in range(heads_here)]
    totals = [[] for member in range(heads_here)]
    for fraction, dilation in zip(FRACTIONS, DILATIONS):
        segment = total_rows // fraction
        per_segment = segment // dilation
        count = rows_here // dilation
        shaped = qkv.reshape(count, dilation, heads_here, 3, head_dim)
        offsets = []
        chosen = []
        for member in range(heads_here):
            offset = (first_head + member) % dilation
            offsets.append(offset)
            chosen.append(
                lax.dynamic_index_in_dim(shaped[:, :, member], offset, axis=1, keepdims=False)
            )
        chosen = jnp.stack(chosen, axis=1)
        queries = chosen[:, :, 0]
        pairs = chosen[:, :, 1:]
        if segment > rows_here:
            levels = (segment // rows_here).bit_length() - 1
            flat_rows = collect_segment(pairs.reshape(count, -1), levels, seq_index)
            pairs = flat_rows.reshape(per_segment, heads_here, 2, head_dim)
            groups = 1
        else:
            groups = rows_here // segment
        grouped_queries = queries.reshape(groups, count // groups, heads_here, head_dim)
        grouped_pairs = pairs.reshape(groups, per_segment, heads_here, 2, head_dim)
        for member in range(heads_here):
            head_out, log_total = lax.map(
                lambda block_in: attend(block_in[0], block_in[1][:, 0], block_in[1][:, 1]),
                (grouped_queries[:, :, member], grouped_pairs[:, :, member]),
            )
            full_out, full_total = expand_rows(
                head_out.reshape(count, head_dim),
                log_total.reshape(count),
                offsets[member],
                dilation,
            )
            outputs[member].append(full_out)
            totals[member].append(full_total)
    merged = [
        merge_scales(outputs[member], totals[member]).astype(jnp.bfloat16)
        for member in range(heads_here)
    ]
    attention = jnp.stack(merged, axis=1).reshape(rows_here, heads_here * head_dim)
    regrouped = lax.all_to_all(attention, "head", split_axis=0, concat_axis=1, tiled=True)
    branch = jnp.dot(
        regrouped,
        lax.all_gather(out_weight, "head", axis=0, tiled=True),
        preferred_element_type=jnp.float32,
    )
    return (embedded + branch).astype(jnp.bfloat16)


MESH = pl.DeviceIdType.MESH
LOWEST = -1e30


def dot_nt(a, b):
    return lax.dot_general(a, b, (((1,), (1,)), ((), ())), preferred_element_type=jnp.float32)


def dot(a, b):
    return jnp.dot(a, b, preferred_element_type=jnp.float32)


def iota(shape, dim):
    return lax.broadcasted_iota(jnp.int32, shape, dim)


def layer_kernel(
    dims,
    tile_any,
    route_ref,
    embed_any,
    gain_ref,
    w_any,
    wo_any,
    out_ref,
    tile_v,
    embed_v,
    wt,
    wo_v,
    outgoing,
    arrived,
    slot_out,
    slot_in,
    emb,
    qs,
    kvs,
    kv2,
    kx3,
    kv3,
    num,
    top,
    den,
    load_sem,
    local_sem,
    w_send,
    w_recv,
    route_send,
    route_recv,
    slot_send,
    slot_recv,
    kv2_send,
    kv2_recv,
    kx3_send,
    kx3_recv,
    kv3_send,
    kv3_recv,
):
    S, H, R, D, NC, M, E, SH, d2, d3 = dims
    cap = arrived.shape[2]
    cols = arrived.shape[3]
    G = M * E
    p2 = R // d2
    p3 = R // d3
    v_low = G // 128 * 128
    VW = 2 * G - v_low
    lead = G - v_low
    scale = E ** (-0.5)
    s = lax.axis_index("seq")
    c = lax.axis_index("head")
    side = lax.axis_index("groups")
    across = 1 - side
    near = c + 1 - 2 * (c % 2)
    far = (c + 2) % H
    near_far = (near + 2) % H
    seq_to = [(s + k) % S for k in range(S)]
    seq_from = [(s + S - k) % S for k in range(S)]

    loads = [pltpu.make_async_copy(tile_any, tile_v, load_sem.at[0])]
    for n in range(NC):
        loads.append(
            pltpu.make_async_copy(
                embed_any.at[:, pl.ds(n * cols, cols)], embed_v.at[n], load_sem.at[1 + n]
            )
        )
    for copy in loads:
        copy.start()

    barrier = pltpu.get_barrier_semaphore()
    for k in range(1, S):
        pl.semaphore_signal(barrier, inc=1, device_id={"seq": seq_to[k]}, device_id_type=MESH)
    for peer in (near, far):
        pl.semaphore_signal(barrier, inc=1, device_id={"head": peer}, device_id_type=MESH)
    pl.semaphore_signal(barrier, inc=1, device_id={"groups": across}, device_id_type=MESH)

    dest = route_ref[0:1, :]
    slot = route_ref[1:2, :]
    sub = max(8, S)
    hits = iota((sub, R), 0) == dest
    hits_f = jnp.where(hits, 1.0, 0.0)
    below = jnp.where(iota((R, R), 0) < iota((R, R), 1), 1.0, 0.0).astype(jnp.bfloat16)
    earlier = dot(hits_f.astype(jnp.bfloat16), below)
    rank = jnp.sum(earlier * hits_f, axis=0, keepdims=True).astype(jnp.int32)
    place = dest * cap + rank
    pick = jnp.where(iota((S * cap, R), 0) == place, 1.0, 0.0).astype(jnp.bfloat16)
    slot_f = jnp.broadcast_to((slot + 1).astype(jnp.float32), (8, R)).astype(jnp.bfloat16)
    slot_rows = dot_nt(slot_f, pick).astype(jnp.int32)
    for t in range(S):
        slot_out[t] = slot_rows[:, t * cap : (t + 1) * cap]

    pl.semaphore_wait(barrier, S - 1 + 3)

    def remote(src, dst, send, recv, **device):
        copy = pltpu.make_async_remote_copy(
            src_ref=src,
            dst_ref=dst,
            send_sem=send,
            recv_sem=recv,
            device_id=device,
            device_id_type=MESH,
        )
        return copy

    slot_copies = []
    for k in range(1, S):
        copy = remote(
            slot_out.at[seq_to[k]], slot_in.at[s], slot_send.at[k], slot_recv.at[k], seq=seq_to[k]
        )
        copy.start()
        slot_copies.append(copy)
    slot_in[s] = slot_out[s]

    half_m, half_g = M // 2, G // 2

    def w_block(owner, x):
        return wt.at[owner, x] if x < 3 else wo_v.at[owner]

    def w_half(owner, x, part):
        if x < 3:
            return wt.at[owner, x, pl.ds(part * half_m, half_m)]
        return wo_v.at[owner, pl.ds(pl.multiple_of(part * half_g, half_g), half_g)]

    def w_copy(source, target, stage, x, **device):
        return remote(source, target, w_send.at[stage, x], w_recv.at[stage, x], **device)

    w_far, w_near, w_local, w_over, w_pass, w_rest = [], [], [], [], [], []
    w_over_in, w_pass_in, w_rest_in = [], [], []
    for x in range(4):
        if x < 3:
            own, own_half = w_any.at[:, x], w_any.at[pl.ds(side * half_m, half_m), x]
        else:
            own = wo_any
            own_half = wo_any.at[pl.ds(pl.multiple_of(side * half_g, half_g), half_g)]
        w_far.append(w_copy(own_half, w_half(c, x, side), 0, x, head=far))
        w_near.append(w_copy(own, w_block(c, x), 1, x, head=near))
        w_local.append(pltpu.make_async_copy(own, w_block(c, x), local_sem.at[x]))
        ref = w_half(far, x, side)
        w_over.append(w_copy(ref, ref, 2, x, groups=across))
        w_pass.append(w_copy(ref, ref, 3, x, head=near))
        ref = w_half(far, x, across)
        w_over_in.append(w_copy(ref, ref, 2, x, groups=across))
        w_rest.append(w_copy(ref, ref, 4, x, head=near))
        ref = w_half(near_far, x, side)
        w_pass_in.append(w_copy(ref, ref, 3, x, head=near))
        ref = w_half(near_far, x, across)
        w_rest_in.append(w_copy(ref, ref, 4, x, head=near))

    def w_first(x):
        w_far[x].wait_recv()
        w_over[x].start()
        w_pass[x].start()

    def w_second(x):
        w_over_in[x].wait_recv()
        w_rest[x].start()

    def w_ready(x):
        w_local[x].wait()
        w_near[x].wait_recv()
        w_pass_in[x].wait_recv()
        w_rest_in[x].wait_recv()

    for x in (1, 2, 0, 3):
        w_far[x].start()
    loads[0].wait()
    route_copies = []
    for n in range(NC):
        loads[1 + n].wait()
        projected = dot(tile_v[...], embed_v[n]).astype(jnp.bfloat16)
        outgoing[n] = dot(pick, projected).astype(jnp.bfloat16).reshape(S, cap, cols)
        row = []
        for k in range(1, S):
            copy = remote(
                outgoing.at[n, seq_to[k]],
                arrived.at[n, s],
                route_send.at[n, k],
                route_recv.at[n, k],
                seq=seq_to[k],
            )
            copy.start()
            row.append(copy)
        route_copies.append(row)
        arrived[n, s] = outgoing[n, s]
    for x in (1, 2, 0, 3):
        w_local[x].start()
        w_near[x].start()

    def original(position):
        return (position % p3) * d3 + ((position // p3) % (d3 // d2)) * d2 + position // p2

    for copy in slot_copies:
        copy.wait_recv()
    slots = jnp.concatenate([slot_in[t][0:1, :] for t in range(S)], axis=1)
    landing = jnp.where(original(iota((R, S * cap), 0)) + 1 == slots, 1.0, 0.0).astype(jnp.bfloat16)
    back = jnp.where(original(iota((R, R), 1)) == iota((R, R), 0), 1.0, 0.0).astype(jnp.bfloat16)

    w_first(1)
    w_first(2)
    w_second(1)
    w_first(0)
    w_second(2)
    w_second(0)
    parts = []
    for n in range(NC):
        for copy in route_copies[n]:
            copy.wait_recv()
        parts.append(dot(landing, arrived[n].reshape(S * cap, cols)))
    embedded = jnp.concatenate(parts, axis=1)
    emb[...] = embedded.astype(jnp.bfloat16)
    normed = layer_norm(embedded, gain_ref[...].reshape(1, D))

    w_ready(1)
    w_ready(2)
    lane_head = (iota((p2, 2 * G), 1) % G) // E
    for g in range(SH):
        kv = dot_nt(normed, wt[g, 1:3].reshape(2 * G, D))
        kvs[g] = kv.astype(jnp.bfloat16)
        chosen = kv[0:p2]
        for m in range(1, M):
            chosen = jnp.where(lane_head == m, kv[m * p2 : (m + 1) * p2], chosen)
        chosen = chosen.astype(jnp.bfloat16)
        kv2[c, g] = chosen
        kx3[g] = chosen[g * p3 : (g + 1) * p3]
    kv2_far = remote(kv2.at[c], kv2.at[c], kv2_send.at[0], kv2_recv.at[0], head=far)
    kv2_near = remote(kv2.at[c], kv2.at[c], kv2_send.at[1], kv2_recv.at[1], head=near)
    kv2_relay = remote(kv2.at[far], kv2.at[far], kv2_send.at[2], kv2_recv.at[2], head=near)
    kv2_relay_in = remote(
        kv2.at[near_far], kv2.at[near_far], kv2_send.at[2], kv2_recv.at[2], head=near
    )
    kx3_copies = []
    for k in range(1, S):
        copy = remote(kx3, kv3.at[s, c], kx3_send.at[k], kx3_recv.at[k], seq=seq_to[k])
        copy.start()
        kx3_copies.append(copy)
    kv2_far.start()
    kv2_near.start()
    w_first(3)
    w_ready(0)
    for g in range(SH):
        qs[g] = dot_nt(normed, wt[g, 0].reshape(G, D)).astype(jnp.bfloat16)

    q_head = iota((R, G), 1) // E
    v_head = (iota((R, VW), 1) - lead + 2 * E) // E - 2

    def scale_one(g, carry):
        queries = qs[g]
        keys = kvs[g, :, 0:G]
        values = kvs[g, :, v_low : 2 * G]
        numer = jnp.zeros((R, VW), jnp.float32)
        peak = jnp.zeros((R, VW), jnp.float32)
        denom = jnp.ones((R, VW), jnp.float32)
        for m in range(M):
            mask = jnp.where(q_head == m, 1.0, 0.0).astype(jnp.bfloat16)
            scores = dot_nt(queries * mask, keys)
            row_max = jnp.max(scores, axis=-1, keepdims=True)
            expo = jnp.exp((scores - row_max) * scale)
            total = jnp.sum(expo, axis=-1, keepdims=True)
            head_out = dot(expo.astype(jnp.bfloat16), values)
            mine = v_head == m
            numer = jnp.where(mine, head_out, numer)
            peak = jnp.where(mine, row_max, peak)
            denom = jnp.where(mine, total, denom)
        num[g] = numer
        top[g] = peak
        den[g] = denom
        return carry

    lax.fori_loop(0, SH - 1, scale_one, 0)
    w_second(3)
    kv2_far.wait_recv()
    kv2_relay.start()
    kv3_far, kv3_near, kv3_relay, kv3_relay_in = [], [], [], []
    for k in range(1, S):
        kx3_copies[k - 1].wait_recv()
        block = kv3.at[seq_from[k], c]
        kv3_far.append(remote(block, block, kv3_send.at[0, k], kv3_recv.at[0, k], head=far))
        kv3_near.append(remote(block, block, kv3_send.at[1, k], kv3_recv.at[1, k], head=near))
        kv3_far[-1].start()
        kv3_near[-1].start()
        block = kv3.at[seq_from[k], far]
        kv3_relay.append(remote(block, block, kv3_send.at[2, k], kv3_recv.at[2, k], head=near))
        block = kv3.at[seq_from[k], near_far]
        kv3_relay_in.append(remote(block, block, kv3_send.at[2, k], kv3_recv.at[2, k], head=near))
    lax.fori_loop(SH - 1, SH, scale_one, 0)

    kv2_near.wait_recv()
    kv2_relay_in.wait_recv()

    def merge(g, rows, mine, row_max, total, head_out):
        old = top[g, rows, :]
        this = jnp.where(mine, row_max, LOWEST)
        peak = jnp.maximum(old, this)
        keep = jnp.exp((old - peak) * scale)
        add = jnp.where(mine, jnp.exp((this - peak) * scale), 0.0)
        top[g, rows, :] = peak
        num[g, rows, :] = num[g, rows, :] * keep + head_out * add
        den[g, rows, :] = den[g, rows, :] * keep + total * add

    q_diag = jnp.where(q_head == iota((R, G), 0) // p2, 1.0, 0.0).astype(jnp.bfloat16)
    v_diag = v_head == iota((R, VW), 0) // p2

    def scale_two(g, carry):
        keys = kv2[:, g, :, 0:G].reshape(H * p2, G)
        values = kv2[:, g, :, v_low : 2 * G].reshape(H * p2, VW)
        scores = dot_nt(qs[g] * q_diag, keys)
        row_max = jnp.max(scores, axis=-1, keepdims=True)
        expo = jnp.exp((scores - row_max) * scale)
        total = jnp.sum(expo, axis=-1, keepdims=True)
        head_out = dot(expo.astype(jnp.bfloat16), values)
        merge(g, pl.ds(0, R), v_diag, row_max, total, head_out)
        return carry

    lax.fori_loop(0, SH, scale_two, 0)
    for k in range(1, S):
        kv3_far[k - 1].wait_recv()
        kv3_relay[k - 1].start()
    for g in range(SH):
        for other in range(H):
            kv3[s, other, g] = kv2[other, g, g * p3 : (g + 1) * p3, :]
    residual = dot(back, emb[...])
    for k in range(1, S):
        kv3_near[k - 1].wait_recv()
        kv3_relay_in[k - 1].wait_recv()

    q_small = jnp.where(
        iota((M * p3, G), 1) // E == iota((M * p3, G), 0) // p3, 1.0, 0.0
    ).astype(jnp.bfloat16)

    def scale_three(g, carry):
        starts = [pl.multiple_of(m * p2 + g * p3, p3) for m in range(M)]
        queries = jnp.concatenate([qs[g, pl.ds(start, p3), :] for start in starts], axis=0)
        keys = kv3[:, :, g, :, 0:G].reshape(S * H * p3, G)
        values = kv3[:, :, g, :, v_low : 2 * G].reshape(S * H * p3, VW)
        scores = dot_nt(queries * q_small, keys)
        row_max = jnp.max(scores, axis=-1, keepdims=True)
        expo = jnp.exp((scores - row_max) * scale)
        total = jnp.sum(expo, axis=-1, keepdims=True)
        head_out = dot(expo.astype(jnp.bfloat16), values)
        for m in range(M):
            part = slice(m * p3, (m + 1) * p3)
            merge(
                g,
                pl.ds(starts[m], p3),
                (iota((p3, VW), 1) >= lead + m * E) & (iota((p3, VW), 1) < lead + (m + 1) * E),
                row_max[part],
                total[part],
                head_out[part],
            )
        return carry

    lax.fori_loop(0, SH, scale_three, 0)

    w_ready(3)
    mixed = residual
    for g in range(SH):
        attention = (num[g] / den[g]).astype(jnp.bfloat16)
        ordered = dot(back, attention)[:, lead:VW].astype(jnp.bfloat16)
        mixed = mixed + dot(ordered, wo_v[g])
    out_ref[...] = mixed.astype(jnp.bfloat16)

    sent = slot_copies + w_far + w_near + w_over + w_pass + w_rest + [kv2_far, kv2_near, kv2_relay] + kx3_copies
    sent += kv3_far + kv3_near + kv3_relay
    for row in route_copies:
        sent += row
    for copy in sent:
        copy.wait_send()


def fused(tile_rows, tile_route, embed_weight, norm_gain, qkv_weight, out_weight):
    S = lax.axis_size("seq")
    H = lax.axis_size("head")
    R, d_in = tile_rows.shape
    D = embed_weight.shape[1]
    M, E = qkv_weight.shape[1], qkv_weight.shape[3]
    G = M * E
    cap = 2 * R // S
    NC = D // 256
    SH = H
    d2, d3 = DILATIONS[1:]
    p2, p3 = R // d2, R // d3
    VW = 2 * G - G // 128 * 128
    bf, f32 = jnp.bfloat16, jnp.float32
    any_spec = pl.BlockSpec(memory_space=pl.ANY)
    vmem = pl.BlockSpec(memory_space=pltpu.VMEM)
    dma = pltpu.SemaphoreType.DMA
    return pl.pallas_call(
        functools.partial(layer_kernel, (S, H, R, D, NC, M, E, SH, d2, d3)),
        out_shape=jax.ShapeDtypeStruct((R, D), bf),
        in_specs=[any_spec, vmem, any_spec, vmem, any_spec, any_spec],
        out_specs=vmem,
        scratch_shapes=[
            pltpu.VMEM((R, d_in), bf),
            pltpu.VMEM((NC, d_in, 256), bf),
            pltpu.VMEM((H, 3, M, E, D), bf),
            pltpu.VMEM((H, G, D), bf),
            pltpu.VMEM((NC, S, cap, 256), bf),
            pltpu.VMEM((NC, S, cap, 256), bf),
            pltpu.VMEM((S, 8, cap), jnp.int32),
            pltpu.VMEM((S, 8, cap), jnp.int32),
            pltpu.VMEM((R, D), bf),
            pltpu.VMEM((SH, R, G), bf),
            pltpu.VMEM((SH, R, 2 * G), bf),
            pltpu.VMEM((H, SH, p2, 2 * G), bf),
            pltpu.VMEM((SH, p3, 2 * G), bf),
            pltpu.VMEM((S, H, SH, p3, 2 * G), bf),
            pltpu.VMEM((SH, R, VW), f32),
            pltpu.VMEM((SH, R, VW), f32),
            pltpu.VMEM((SH, R, VW), f32),
            dma((1 + NC,)),
            dma((4,)),
            dma((5, 4)),
            dma((5, 4)),
            dma((NC, S)),
            dma((NC, S)),
            dma((S,)),
            dma((S,)),
            dma((3,)),
            dma((3,)),
            dma((S,)),
            dma((S,)),
            dma((3, S)),
            dma((3, S)),
        ],
        compiler_params=pltpu.CompilerParams(
            collective_id=0, has_side_effects=True, vmem_limit_bytes=56 * 1024 * 1024
        ),
    )(
        tile_rows,
        tile_route.T,
        embed_weight,
        norm_gain,
        qkv_weight.transpose(1, 2, 3, 0),
        out_weight,
    )


def fits(mesh):
    def check(tile_rows, embed_weight, qkv_weight):
        S, H = mesh.shape["seq"], mesh.shape["head"]
        rows = tile_rows.shape[0] // mesh.size
        heads = qkv_weight.shape[1] // H
        d2, d3 = DILATIONS[1:]
        return (
            H == 4
            and mesh.shape["groups"] == 2
            and heads == d2
            and heads * H == d3
            and FRACTIONS[0] == S * H
            and FRACTIONS[1] == S
            and FRACTIONS[2] == 1
            and rows % (16 * d3) == 0
            and rows <= 256
            and embed_weight.shape[1] % 256 == 0
            and embed_weight.shape[1] // 256 >= 3
        )

    return check


def solution(mesh):
    check = fits(mesh)

    def program(tile_rows, tile_route, embed_weight, norm_gain, qkv_weight, out_weight):
        body = fused if check(tile_rows, embed_weight, qkv_weight) else local
        return jax.shard_map(
            body,
            mesh=mesh,
            in_specs=(
                P(("groups", "seq", "head"), None),
                P(("groups", "seq", "head"), None),
                P(),
                P(),
                P(None, "head", None, None),
                P("head", None),
            ),
            out_specs=P(("groups", "seq", "head"), None),
            check_vma=False,
        )(tile_rows, tile_route, embed_weight, norm_gain, qkv_weight, out_weight)

    return program
```
